256 devices in a mesh: group: 8 (over y, core), leaf: 32 (over z, x).
Axes of the slice: x: 4, y: 4, z: 8, core: 2. Of those that a mesh axis runs over, the one named last changes fastest.
Arguments:
- points: float32 [3, 524288], P(None, ('group', 'leaf')), may hold values from 0 to 1
- rhs: float32 [16, 524288], P(None, ('group', 'leaf')), may hold values from -0.5 to 0.5
- counts: int32 [4096], P(('group', 'leaf')), may hold values from 32 to 128
- basis: float32 [4096, 128, 32], P(('group', 'leaf')), may hold values from -1 to 1
- leaf_geom: float32 [4096, 4], P(('group', 'leaf')), may hold values from 0.05 to 1
- leaf_partners: int32 [4096, 16], P(('group', 'leaf')), may hold values from -16 to 16, as said below
- leaf_middle_owner: int32 [256, 16], P(('group', 'leaf')), may hold values from 0 to 7, never falling along the last dimension, each value on 1 to 4 neighbouring positions
- leaf_basis_transfer: float32 [4096, 32, 32], P(('group', 'leaf')), may hold values from -1 to 1
- mid_geom: float32 [2048, 4], P(('group', 'leaf')), may hold values from 0.05 to 1
- mid_parent: int32 [8, 256], P('group', 'leaf'), may hold values from 0 to 15, never falling along the last dimension, each value on 1 to 32 neighbouring positions
- mid_transfer: float32 [2048, 32, 32], P(('group', 'leaf')), may hold values from -1 to 1
- mid_peers: int32 [2048, 8], P(('group', 'leaf')), may hold values from 0 to 31, all different within a row; in each aligned block of 8 rows (0 to 7, 8 to 15, ...) at most 4 rows name the same one
- mid_slots: int32 [2048, 8], P(('group', 'leaf')), may hold values from 0 to 7
- top_geom: float32 [128, 4], P('group'), may hold values from 0.05 to 1
- top_offsets: int32 [128, 16], P('group'), may hold values from 1 to 127
Outputs:
- product: float32 [16, 524288], P(None, ('group', 'leaf'))
The draws below stay inside these ranges and needn't reach their ends.
Inputs may be any that keep to these rules, and one draw needn't show every extreme that they name: `leaf_partners`: column 0 is 0. Every partner leaf lies in the same group, at most 16 leaves away. `mid_peers`: over the rows of one device, no device is named more than 4 times, and some device is named exactly 4 times; the names in a row differ. `leaf_middle_owner`: never falling along a row. `mid_parent`: never falling along a row.
All inputs are finite; a program needn't handle non-finite values.
Results may differ from the reference program's by a relative error of at most 0.00013.
Values sent between devices are 32-bit elements; how exact they have to be, the bound alone decides.
A program may use at most 64 MiB of HBM per device.

```python
import math
import jax
import jax.numpy as jnp
import numpy as np
from jax import lax

PTS = 128
RANK = 32
RHS = 16
LEAF_DEV = 16
MID_DEV = 8
TOP = 16
NEAR = 8
FAR = 8
REACH = 16
IL_MID = 8
IL_TOP = 16
LG = 512
MG = 256
LEAVES = 4096
POINTS = 524288
MIDS = 2048
TOPS = 128
CAP = 4
N_GROUP = 8
N_LEAF = 32


def draw_leaf_partners(key, part):
    leaf_total = LEAF_DEV * N_GROUP * N_LEAF
    options_count = 2 * REACH
    scores = jax.random.randint(key, (leaf_total, options_count), 0, 1 << 20) * options_count + jnp.arange(options_count, dtype=jnp.int32)[None, :]
    ranking = jnp.argsort(scores, axis=1)
    candidate = jnp.concatenate([jnp.arange(-REACH, 0, dtype=jnp.int32), jnp.arange(1, REACH + 1, dtype=jnp.int32)])
    picked = candidate[ranking[:, :NEAR + FAR - 1]]
    within = (jnp.arange(leaf_total, dtype=jnp.int32) % LG)[:, None]
    landing = within + picked
    picked = jnp.where((landing < 0) | (landing >= LG), -picked, picked)
    return jnp.concatenate([jnp.zeros((leaf_total, 1), jnp.int32), picked.astype(jnp.int32)], axis=1)


def plant(values, own_key, least, high):
    place = [jax.random.randint(jax.random.fold_in(own_key, axis), (), 0, length) for axis, length in enumerate(values.shape)]
    widest = values.shape.index(max(values.shape))
    next_to = place[:widest] + [(place[widest] + 1) % values.shape[widest]] + place[widest + 1:]
    return values.at[tuple(place)].set(least).at[tuple(next_to)].set(high)


def steps_of(stream_key, shape, shards, low, top_value):
    loudness = 1.0
    for dim, blocks in shards:
        heights = jax.random.uniform(jax.random.fold_in(jax.random.fold_in(stream_key, 6), dim), (blocks,), jnp.float32, low / len(shards), top_value / len(shards))
        loudness = loudness * jnp.repeat(jnp.exp(heights), shape[dim] // blocks).reshape((-1,) + (1,) * (len(shape) - 1 - dim))
    return loudness


def profile(count, total, bound, slope):
    weights = [(1 << 20) // math.isqrt(rank ** slope) + 1 for rank in range(2, count + 1)]
    spare, holding = total - bound - (count - 1), [1] * (count - 1)
    while spare > 0:
        movable = [i for i in range(count - 1) if holding[i] < bound]
        mass, remaining = sum([weights[i] for i in movable]), spare
        for i in movable:
            more = min(bound - holding[i], max(1, remaining * weights[i] // mass), spare)
            holding[i] = holding[i] + more
            spare = spare - more
    return np.array([bound] + holding)


def uneven_parts(key, number_of, total, most, slope):
    if number_of == 2:
        one = jax.random.randint(key, (), max(1, total - most), min(most, total - 1) + 1)
        return jnp.stack([one, total - one])
    lengths = jnp.asarray(profile(number_of, total, most, slope), jnp.int32)
    couples = (number_of - 1) // 2
    source_of, sink = lengths[1:1 + 2 * couples:2], lengths[2:2 + 2 * couples:2]
    margin = jnp.minimum(source_of - 1, most - sink)
    shifted = jax.random.randint(jax.random.fold_in(key, 1), (couples,), 0, 1 << 20) % (margin + 1)
    lengths = lengths.at[1:1 + 2 * couples:2].set(source_of - shifted).at[2:2 + 2 * couples:2].set(sink + shifted)
    return lengths[jax.random.permutation(jax.random.fold_in(key, 2), number_of)]


def assign_block(own_key, own, number, rows, amount, top, most, skew):
    order = jax.random.permutation(own_key, amount)
    packed, common = portions_of(amount, rows * top, most, skew, True), portions_of(amount, rows * top, most, skew, False)
    places = jnp.arange(amount)

    def named(lengths, offset_by):
        used = int((lengths > 0).sum())
        fixed = max(1, used // 4)
        passed = fixed + (places - fixed + offset_by * (used - fixed)) % max(1, amount - fixed)
        return jnp.zeros((amount,), jnp.int32).at[order[jnp.where(places < fixed, places, passed)]].set(jnp.asarray(lengths, jnp.int32))

    lengths = jnp.where(number % 4 == 0, named(packed, number // 4), named(common, number - number // 4 - 1))
    mixed = jax.random.permutation(jax.random.fold_in(own, 3), amount)
    source_of, taker = mixed[0:amount // 2 * 2:2], mixed[1:amount // 2 * 2:2]
    slack = jnp.minimum(lengths[source_of] - 1, most - lengths[taker]) // 2
    slack = jnp.where((source_of == order[0]) | (taker == order[0]) | (lengths[taker] == 0), 0, jnp.maximum(slack, 0))
    passed = jax.random.randint(jax.random.fold_in(own, 4), (amount // 2,), 0, 1 << 20) % (slack + 1)
    lengths = lengths.at[source_of].add(-passed).at[taker].add(passed)
    labels = jnp.searchsorted(jnp.cumsum(lengths), jnp.arange(rows * top), side="right").astype(jnp.int32)
    table = labels.reshape(top, rows).T
    table = table[jax.random.permutation(jax.random.fold_in(own, 1), rows)]
    offset_by = jax.random.randint(jax.random.fold_in(own, 2), (rows, 1), 0, top)
    return jnp.take_along_axis(table, (jnp.arange(top)[None, :] + offset_by) % top, axis=1)


def portions_of(count, total, most, slope, full):
    portions = [(1 << 20) // math.isqrt(standing ** slope) + 1 for standing in range(1, count + 1)]
    largest = most if full else min(most, max(-(-total // count), total * portions[0] // sum(portions)))
    least = 1 if total - largest >= count - 1 else 0
    holding, rest = [largest] + [least] * (count - 1), total - largest - least * (count - 1)
    while rest > 0:
        movable = [i for i in range(1, count) if holding[i] < largest] or [i for i in range(1, count) if holding[i] < most]
        pool, budget = sum([portions[i] for i in movable]), rest
        for i in movable:
            more = min(most - holding[i], max(1, budget * portions[i] // pool), rest)
            holding[i] = holding[i] + more
            rest = rest - more
    return np.array(holding)


def gaussian(stream_key, extent, deviation, bound, shards=(), kind=jnp.bfloat16):
    loudness = steps_of(stream_key, extent, shards, -0.22, 0.18) if shards else 1.0
    values = jax.random.normal(stream_key, extent, jnp.float32) * deviation * loudness
    return jnp.minimum(jnp.maximum(values, -bound), bound).astype(kind)


def setup_inputs(seed: int = 0) -> dict:
    streams_of = jax.random.split(jax.random.key(seed), 16)
    points = jnp.clip(1.0 * jax.random.uniform(streams_of[0], (3, POINTS), jnp.float32) ** steps_of(streams_of[0], (3, POINTS), ((1, 256),), -0.2, 0.2), 0.0, 1.0)
    rhs = gaussian(streams_of[1], (RHS, POINTS), 0.0625, 0.5, ((1, 256),), jnp.float32)
    counts = plant(jax.random.randint(streams_of[2], (LEAVES,), PTS // 4, PTS + 1), jax.random.fold_in(streams_of[2], 1), PTS // 4, PTS).astype(jnp.int32)
    basis = gaussian(streams_of[3], (LEAVES, PTS, RANK), RANK ** -0.5, 1.0, ((0, 256),), jnp.float32)
    leaf_geom = jnp.clip(0.05 + 0.95 * jax.random.uniform(streams_of[4], (LEAVES, 4), jnp.float32) ** steps_of(streams_of[4], (LEAVES, 4), ((0, 256),), -0.2, 0.2), 0.05, 1.0)
    leaf_partners = draw_leaf_partners(jax.random.fold_in(streams_of[15], 71), 0)
    leaf_middle_owner = jax.vmap(lambda own: jnp.searchsorted(jnp.cumsum(uneven_parts(own, MID_DEV, LEAF_DEV, 2 * LEAF_DEV // MID_DEV, 1)), jnp.arange(LEAF_DEV), side="right"))(jax.random.split(streams_of[6], (N_GROUP * N_LEAF))).reshape((N_GROUP * N_LEAF, LEAF_DEV)).astype(jnp.int32)
    leaf_basis_transfer = gaussian(streams_of[7], (LEAVES, RANK, RANK), RANK ** -0.5, 1.0, ((0, 256),), jnp.float32)
    mid_geom = jnp.clip(0.05 + 0.95 * jax.random.uniform(streams_of[8], (MIDS, 4), jnp.float32) ** steps_of(streams_of[8], (MIDS, 4), ((0, 256),), -0.2, 0.2), 0.05, 1.0)
    mid_parent = jax.vmap(lambda own: jnp.searchsorted(jnp.cumsum(uneven_parts(own, TOP, MG, 2 * MG // TOP, 1)), jnp.arange(MG), side="right"))(jax.random.split(streams_of[9], N_GROUP)).reshape((N_GROUP, MG)).astype(jnp.int32)
    mid_transfer = gaussian(streams_of[10], (MIDS, RANK, RANK), RANK ** -0.5, 1.0, ((0, 256),), jnp.float32)
    mid_peers_keys = jax.random.split(jax.random.fold_in(streams_of[11], 1), MIDS // MID_DEV)
    mid_peers_turns = jax.random.permutation(jax.random.fold_in(streams_of[11], 3), MIDS // MID_DEV)
    mid_peers = jax.vmap(lambda own, number: assign_block(jax.random.fold_in(streams_of[11], 2), own, number, MID_DEV, N_LEAF, IL_MID, CAP, 2))(mid_peers_keys, mid_peers_turns).reshape((MIDS, IL_MID))
    mid_slots = plant(jax.random.randint(streams_of[12], (MIDS, IL_MID), 0, MID_DEV), jax.random.fold_in(streams_of[12], 1), 0, MID_DEV - 1).astype(jnp.int32)
    top_geom = jnp.clip(0.05 + 0.95 * jax.random.uniform(streams_of[13], (TOPS, 4), jnp.float32) ** steps_of(streams_of[13], (TOPS, 4), ((0, 8),), -0.2, 0.2), 0.05, 1.0)
    top_offsets = plant(jax.random.randint(streams_of[14], (TOPS, IL_TOP), 1, TOPS), jax.random.fold_in(streams_of[14], 1), 1, TOPS - 1).astype(jnp.int32)
    return {"points": points, "rhs": rhs, "counts": counts, "basis": basis, "leaf_geom": leaf_geom, "leaf_partners": leaf_partners, "leaf_middle_owner": leaf_middle_owner, "leaf_basis_transfer": leaf_basis_transfer, "mid_geom": mid_geom, "mid_parent": mid_parent, "mid_transfer": mid_transfer, "mid_peers": mid_peers, "mid_slots": mid_slots, "top_geom": top_geom, "top_offsets": top_offsets}


exact_product = lax.Precision.HIGHEST
root_three = 1.7320508075688772
length_scale = 0.5

def node_table():
    indices = jnp.arange(RANK, dtype=jnp.int32)
    layers = []
    for axis_number in range(3):
        spread = (indices * (2 * axis_number + 3) % RANK).astype(jnp.float32)
        layers.append(jnp.cos(jnp.pi * (spread + 0.5) / RANK))
    return jnp.stack(layers)

def place_nodes(geometry, table):
    return geometry[..., :3, None] + geometry[..., 3:4, None] * table

def matern(left, right):
    squared = jnp.zeros((), jnp.float32)
    for axis_number in range(3):
        difference = left[..., axis_number, :, None] - right[..., axis_number, None, :]
        squared = squared + difference * difference
    distance = jnp.sqrt(squared)
    decay_rate = root_three / length_scale
    return (1.0 + decay_rate * distance) * jnp.exp(-decay_rate * distance)

def couple(target_nodes, source_nodes, source_coeff):
    coupling = matern(target_nodes[:, None], source_nodes)
    return jnp.einsum('njkm,njmr->nkr', coupling, source_coeff, precision=exact_product)

def reference(points, rhs, counts, basis, leaf_geom, leaf_partners, leaf_middle_owner, leaf_basis_transfer, mid_geom, mid_parent, mid_transfer, mid_peers, mid_slots, top_geom, top_offsets):
    leaf_total = counts.shape[0]
    position = jnp.arange(PTS, dtype=jnp.int32)
    present = (position[None, :] < counts[:, None]).astype(jnp.float32)
    masked = rhs.reshape(RHS, leaf_total, PTS) * present[None]
    point_cloud = points.reshape(3, leaf_total, PTS)
    leaf_coefficient_rows = jnp.einsum('lpk,rlp->lkr', basis, masked, precision=exact_product)
    leaf_index = jnp.arange(leaf_total, dtype=jnp.int32)
    mid_of_leaf = (leaf_index // LEAF_DEV * MID_DEV + leaf_middle_owner.reshape(-1)).astype(jnp.int32)
    mid_total = mid_transfer.shape[0]
    upward_coefficients = jnp.einsum('qcz,qct->qzt', leaf_basis_transfer, leaf_coefficient_rows, precision=exact_product)
    coeff_mid = jax.ops.segment_sum(upward_coefficients, mid_of_leaf, num_segments=mid_total)
    mid_index = jnp.arange(mid_total, dtype=jnp.int32)
    top_of_mid = (mid_index // MG * TOP + mid_parent.reshape(-1)).astype(jnp.int32)
    top_total = top_geom.shape[0]
    raised = jnp.einsum('mkj,mkr->mjr', mid_transfer, coeff_mid, precision=exact_product)
    coeff_top = jax.ops.segment_sum(raised, top_of_mid, num_segments=top_total)
    table = node_table()
    upper_level_nodes = place_nodes(top_geom, table)
    top_source = ((jnp.arange(top_total, dtype=jnp.int32)[:, None] + top_offsets) % top_total).astype(jnp.int32)
    local_top = couple(upper_level_nodes, upper_level_nodes[top_source], coeff_top[top_source])
    mid_nodes = place_nodes(mid_geom, table)
    mid_source = ((mid_index // MG)[:, None] * MG + mid_peers * MID_DEV + mid_slots).astype(jnp.int32)
    device_middle_index = jnp.einsum('mkj,mjr->mkr', mid_transfer, local_top[top_of_mid], precision=exact_product)
    device_middle_index = device_middle_index + couple(mid_nodes, mid_nodes[mid_source], coeff_mid[mid_source])
    leaf_nodes = place_nodes(leaf_geom, table)

    def block(block_start):
        leaf_rows = block_start * LEAF_DEV + jnp.arange(LEAF_DEV, dtype=jnp.int32)
        partner = leaf_rows[:, None] + lax.dynamic_slice_in_dim(leaf_partners, block_start * LEAF_DEV, LEAF_DEV, 0)
        near_ids = partner[:, :NEAR]
        far_ids = partner[:, NEAR:]
        target_cloud = point_cloud[:, leaf_rows].transpose(1, 0, 2)
        source_cloud = point_cloud[:, near_ids].transpose(1, 2, 0, 3)
        kernel = matern(target_cloud[:, None], source_cloud)
        near_part = jnp.einsum('bjpq,rbjq->rbp', kernel, masked[:, near_ids], precision=exact_product)
        far_part = couple(leaf_nodes[leaf_rows], leaf_nodes[far_ids], leaf_coefficient_rows[far_ids])
        local_leaf = jnp.einsum('bkm,bmr->bkr', leaf_basis_transfer[leaf_rows], device_middle_index[mid_of_leaf[leaf_rows]], precision=exact_product) + far_part
        result = jnp.einsum('bpk,bkr->rbp', basis[leaf_rows], local_leaf, precision=exact_product) + near_part
        return result * present[leaf_rows][None]
    blocks = lax.map(block, jnp.arange(leaf_total // LEAF_DEV, dtype=jnp.int32))
    return blocks.transpose(1, 0, 2, 3).reshape(RHS, leaf_total * PTS)
```

```python
import functools

import jax
import jax.numpy as jnp
import numpy as np
from jax import lax
from jax.experimental import pallas as pl
from jax.experimental.pallas import tpu as pltpu
from jax.sharding import PartitionSpec as P

MESH = pl.DeviceIdType.MESH
HI = lax.Precision.HIGHEST
PTS = 128
RANK = 32
RHS = 16
RATE = 1.7320508075688772 / 0.5
NX = 4
NZ = 8
NL = 32
NG = 8


def node_table():
    k = np.arange(RANK)
    rows = [
        np.cos(np.pi * (((k * (2 * d + 3)) % RANK) + 0.5) / RANK) for d in range(3)
    ]
    return np.stack(rows).astype(np.float32)


def nt(a, b, precision=HI):
    return lax.dot_general(
        a,
        b,
        (((1,), (1,)), ((), ())),
        precision=precision,
        preferred_element_type=jnp.float32,
    )


def nn(a, b):
    return lax.dot_general(
        a,
        b,
        (((1,), (0,)), ((), ())),
        precision=HI,
        preferred_element_type=jnp.float32,
    )


def kappa(squared):
    squared = jnp.maximum(squared, 1e-30)
    t = squared * lax.rsqrt(squared)
    return (1.0 + t) * jnp.exp(-t)


def block_of(shape):
    return lax.broadcasted_iota(jnp.int32, shape, 1) >> 5


def up_kernel(counts, owner, parent, rhs, basis, leaf_t, mid_t, masked, leafc, midc, ptop):
    lane = lax.broadcasted_iota(jnp.int32, (RHS, PTS), 1)
    pieces = []
    for l in range(16):
        cols = slice(l * PTS, (l + 1) * PTS)
        m = jnp.where(lane < counts[l], rhs[:, cols], 0.0)
        masked[:, cols] = m
        pieces.append(nt(m, basis[l]))
    row = lax.broadcasted_iota(jnp.int32, (128, 128), 0) >> 4
    blk = block_of((128, 128))
    total = jnp.zeros((128, RANK), jnp.float32)
    for q in range(4):
        tile = jnp.concatenate(pieces[4 * q : 4 * q + 4], axis=1)
        leafc[q] = tile
        own = jnp.full((128, 128), owner[0, 4 * q], jnp.int32)
        for b in range(1, 4):
            own = jnp.where(blk == b, owner[0, 4 * q + b], own)
        lhs = jnp.where(own == row, jnp.concatenate([tile] * 8, axis=0), 0.0)
        total = total + nn(lhs, leaf_t[4 * q : 4 * q + 4].reshape(128, RANK))
    row = lax.broadcasted_iota(jnp.int32, (256, 128), 0) >> 4
    blk = block_of((256, 128))
    tops = jnp.zeros((256, RANK), jnp.float32)
    for q in range(2):
        tile = jnp.concatenate(
            [total[(4 * q + b) * 16 : (4 * q + b + 1) * 16] for b in range(4)], axis=1
        )
        midc[q] = tile
        own = jnp.full((256, 128), parent[0, 4 * q], jnp.int32)
        for b in range(1, 4):
            own = jnp.where(blk == b, parent[0, 4 * q + b], own)
        lhs = jnp.where(own == row, jnp.concatenate([tile] * 16, axis=0), 0.0)
        tops = tops + nn(lhs, mid_t[4 * q : 4 * q + 4].reshape(128, RANK))
    for q in range(4):
        tile = jnp.concatenate(
            [tops[(4 * q + b) * 16 : (4 * q + b + 1) * 16] for b in range(4)], axis=1
        )
        for i in range(8):
            ptop[q * 8 + i] = tile[2 * i : 2 * i + 2]


def comm_kernel(
    masked, points, leafc, midc, ptop, geo, tgeo,
    mhalo, phalo, lhalo, mids, geos, tgeos, tops,
    rsbuf, zbuf,
    s_rs, r_rs, s_h, r_h, s_mid, r_mid, s_geo, r_geo, s_tg, r_tg, s_z, r_z, s_top, r_top,
):
    g = lax.axis_index("group")
    d = lax.axis_index("leaf")
    z = d // NX
    x = d % NX

    def leaf_peer(k):
        return (g, lax.rem(d + k, NL))

    def ring_peer(k):
        return (g, lax.rem(z + k, NZ) * NX + x)

    def plane_peer(k):
        return (lax.rem(g + k // NX, NG), z * NX + lax.rem(x + k % NX, NX))

    barrier = pltpu.get_barrier_semaphore()

    def hello_leaf(k, c):
        pl.semaphore_signal(barrier, inc=1, device_id=leaf_peer(k), device_id_type=MESH)
        return c

    def hello_plane(k, c):
        pl.semaphore_signal(barrier, inc=1, device_id=plane_peer(k), device_id_type=MESH)
        return c

    lax.fori_loop(1, NL, hello_leaf, 0)
    lax.fori_loop(1, 32, hello_plane, 0)
    pl.semaphore_wait(barrier, 62)

    def copy(src, dst, ss, rs, peer):
        return pltpu.make_async_remote_copy(
            src_ref=src, dst_ref=dst, send_sem=ss, recv_sem=rs, device_id=peer, device_id_type=MESH
        )

    def rs_copy(k):
        o = lax.rem(d + k, NL)
        return copy(
            ptop.at[(o % NX) * 8 + o // NX], rsbuf.at[k], s_rs.at[k], r_rs.at[k], leaf_peer(k)
        )

    def geo_copy(k):
        return copy(geo, geos.at[d], s_geo.at[k], r_geo.at[k], leaf_peer(k))

    def mid_copy(k):
        return copy(midc, mids.at[d], s_mid.at[k], r_mid.at[k], leaf_peer(k))

    def tg_copy(k):
        return copy(tgeo, tgeos.at[g], s_tg.at[k], r_tg.at[k], (lax.rem(g + k, NG), d))

    def z_copy(k):
        return copy(zbuf.at[z], zbuf.at[z], s_z.at[k], r_z.at[k], ring_peer(k))

    def top_copy(k):
        return copy(zbuf, tops.at[g * NX + x], s_top.at[k], r_top.at[k], plane_peer(k))

    halo = []
    for side in range(2):
        peer = leaf_peer(NL - 1 if side == 0 else 1)
        slot = 1 - side
        halo.append(copy(points, phalo.at[slot], s_h.at[slot, 0], r_h.at[slot, 0], peer))
        halo.append(copy(masked, mhalo.at[slot], s_h.at[slot, 1], r_h.at[slot, 1], peer))
        halo.append(copy(leafc, lhalo.at[slot], s_h.at[slot, 2], r_h.at[slot, 2], peer))

    def each(lo, hi, f):
        def step(k, c):
            f(k)
            return c

        lax.fori_loop(lo, hi, step, 0)

    each(1, NL, lambda k: rs_copy(k).start())
    each(1, NL, lambda k: geo_copy(k).start())
    each(1, NG, lambda k: tg_copy(k).start())
    for c in halo:
        c.start()
    mids[d] = midc[...]
    geos[d] = geo[...]
    tgeos[g] = tgeo[...]
    each(1, NL, lambda k: rs_copy(k).wait_recv())
    total = ptop[x * 8 + z]
    for k in range(1, NL):
        total = total + rsbuf[k]
    zbuf[z] = total
    each(1, NZ, lambda k: z_copy(k).start())
    each(1, NL, lambda k: mid_copy(k).start())
    each(1, NZ, lambda k: z_copy(k).wait_recv())
    each(1, 32, lambda k: top_copy(k).start())
    tops[g * NX + x] = zbuf[...]
    each(1, NL, lambda k: mid_copy(k).wait_recv())
    each(1, NL, lambda k: geo_copy(k).wait_recv())
    each(1, NG, lambda k: tg_copy(k).wait_recv())
    for c in halo:
        c.wait_recv()
    each(1, 32, lambda k: top_copy(k).wait_recv())
    each(1, NL, lambda k: rs_copy(k).wait_send())
    each(1, NL, lambda k: geo_copy(k).wait_send())
    each(1, NG, lambda k: tg_copy(k).wait_send())
    each(1, NZ, lambda k: z_copy(k).wait_send())
    each(1, NL, lambda k: mid_copy(k).wait_send())
    each(1, 32, lambda k: top_copy(k).wait_send())
    for c in halo:
        c.wait_send()


def down_kernel(
    counts, owner, parent, partners, peers, slots, offsets, geos, tgeos,
    masked, points, leafc, mhalo, phalo, lhalo, mids, tops, basis, leaf_t, mid_t, trow, tcol,
    out,
    mhl, pts, lwin, mid_s, tb, far_s,
):
    g = lax.axis_index("group")
    d = lax.axis_index("leaf")
    blk16 = block_of((RHS, 128))
    blk1 = block_of((1, 128))

    def gather(tab, srcs):
        acc = None
        for j, s in enumerate(srcs):
            t = pltpu.roll(tab[s >> 2], ((j - (s & 3)) & 3) * 32, 1)
            acc = t if j == 0 else jnp.where(blk16 == j, t, acc)
        return acc

    def target_nodes(read):
        h = read(3)
        return [(read(c) + h * tcol[c]) * RATE for c in range(3)]

    def coupling(tnodes, reads):
        def mix(c):
            v = jnp.full((1, 128), reads[0](c), jnp.float32)
            for j in range(1, 4):
                v = jnp.where(blk1 == j, reads[j](c), v)
            return v

        h = mix(3)
        squared = None
        for c in range(3):
            row = (mix(c) + h * trow[c : c + 1, :]) * RATE
            diff = tnodes[c] - row
            squared = diff * diff if squared is None else squared + diff * diff
        return kappa(squared)

    def top_read(s):
        return lambda c: tgeos[s >> 4, c * 16 + (s & 15)]

    def mid_read(i):
        return lambda c: geos[i >> 3, c * 8 + (i & 7)]

    def leaf_read(w):
        dev = lax.rem(d + NL - 1 + (w >> 4), NL)
        return lambda c: geos[dev, 32 + c * 16 + (w & 15)]

    def window(i, carry):
        cols = pl.ds(pl.multiple_of(i * PTS, PTS), PTS)
        for part in range(3):
            if part == 1:
                m, p = masked[:, cols], points[:, cols]
            else:
                m, p = mhalo[part // 2, :, cols], phalo[part // 2, :, cols]
            high = m.astype(jnp.bfloat16)
            low = (m - high.astype(jnp.float32)).astype(jnp.bfloat16)
            mhl[part * 16 + i] = jnp.concatenate([high, low], axis=0)
            pts[part * 16 + i, 0:3] = p * RATE
        return carry

    pts[...] = jnp.zeros_like(pts)
    lax.fori_loop(0, 16, window, 0)
    lwin[0:4] = lhalo[0]
    lwin[4:8] = leafc[...]
    lwin[8:12] = lhalo[1]

    def mid_step(b, carry):
        p = parent[0, b]
        t = g * 16 + p
        nodes = target_nodes(top_read(t))
        cs, ss = [], []
        for q in range(4):
            srcs = [(t + offsets[p, 4 * q + j]) & 127 for j in range(4)]
            cs.append(gather(tops, srcs))
            ss.append(coupling(nodes, [top_read(s) for s in srcs]))
        local = nt(jnp.concatenate(cs, axis=1), jnp.concatenate(ss, axis=1))
        nodes = target_nodes(mid_read(d * 8 + b))
        cs, ss = [], []
        for q in range(2):
            srcs = [peers[b, 4 * q + j] * 8 + slots[b, 4 * q + j] for j in range(4)]
            cs.append(gather(mids, srcs))
            ss.append(coupling(nodes, [mid_read(s) for s in srcs]))
        mid_s[b] = nt(local, mid_t[b]) + nt(
            jnp.concatenate(cs, axis=1), jnp.concatenate(ss, axis=1)
        )
        return carry

    lax.fori_loop(0, 8, mid_step, 0)

    def leaf_step(l, carry):
        nodes = target_nodes(leaf_read(l + 16))
        cs, ss = [], []
        for q in range(2):
            srcs = [l + 16 + partners[l, 8 + 4 * q + j] for j in range(4)]
            cs.append(gather(lwin, srcs))
            ss.append(coupling(nodes, [leaf_read(s) for s in srcs]))
        local = nt(mid_s[owner[0, l]], leaf_t[l]) + nt(
            jnp.concatenate(cs, axis=1), jnp.concatenate(ss, axis=1)
        )
        far_s[l] = nn(local, basis[l])
        return carry

    lax.fori_loop(0, 16, leaf_step, 0)
    lane = lax.broadcasted_iota(jnp.int32, (RHS, PTS), 1)

    def near_step(l, carry):
        target = pts[l + 16].T
        for c in range(3):
            tb[c] = jnp.broadcast_to(target[:, c : c + 1], (PTS, PTS))
        both = jnp.zeros((PTS, 2 * RHS), jnp.float32)
        rest = jnp.zeros((PTS, RHS), jnp.float32)
        for j in range(0, 8, 2):
            highs, lows, ms = [], [], []
            for e in range(2):
                w = l + 16 + partners[l, j + e]
                squared = None
                for c in range(3):
                    diff = tb[c] - pts[w, c : c + 1, :]
                    squared = diff * diff if squared is None else squared + diff * diff
                k = kappa(squared)
                high = k.astype(jnp.bfloat16)
                highs.append(high)
                lows.append((k - high.astype(jnp.float32)).astype(jnp.bfloat16))
                ms.append(mhl[w])
            m = jnp.concatenate(ms, axis=1)
            both = both + nt(jnp.concatenate(highs, axis=1), m, None)
            rest = rest + nt(jnp.concatenate(lows, axis=1), m[:RHS], None)
        near = both[:, :RHS] + both[:, RHS:] + rest
        cols = pl.ds(pl.multiple_of(l * PTS, PTS), PTS)
        out[:, cols] = jnp.where(lane < counts[l], near.T + far_s[l], 0.0)
        return carry

    lax.fori_loop(0, 16, near_step, 0)


VM = pl.BlockSpec(memory_space=pltpu.VMEM)
SM = pl.BlockSpec(memory_space=pltpu.SMEM)


def f32(*shape):
    return jax.ShapeDtypeStruct(shape, jnp.float32)


def on_device(
    points, rhs, counts, basis, leaf_geom, leaf_partners, leaf_middle_owner, leaf_basis_transfer,
    mid_geom, mid_parent, mid_transfer, mid_peers, mid_slots, top_geom, top_offsets,
):
    basis_t = jnp.swapaxes(basis, 1, 2)
    masked, leafc, midc, ptop = pl.pallas_call(
        up_kernel,
        out_shape=(f32(16, 2048), f32(4, 16, 128), f32(2, 16, 128), f32(32, 2, 128)),
        in_specs=[SM] * 3 + [VM] * 4,
        out_specs=(VM,) * 4,
        name="up",
    )(counts, leaf_middle_owner, mid_parent, rhs, basis_t, leaf_basis_transfer, mid_transfer)
    geo = jnp.concatenate(
        [mid_geom.T.reshape(32), leaf_geom.T.reshape(64), jnp.zeros((32,), jnp.float32)]
    )[None]
    tgeo = jnp.concatenate([top_geom.T.reshape(64), jnp.zeros((64,), jnp.float32)])[None]
    dma = pltpu.SemaphoreType.DMA
    mhalo, phalo, lhalo, mids, geos, tgeos, tops = pl.pallas_call(
        comm_kernel,
        out_shape=(
            f32(2, 16, 2048), f32(2, 3, 2048), f32(2, 4, 16, 128), f32(32, 2, 16, 128),
            f32(32, 1, 128), f32(8, 1, 128), f32(32, 8, 2, 128),
        ),
        in_specs=[VM] * 7,
        out_specs=(VM,) * 7,
        scratch_shapes=[
            pltpu.VMEM((32, 2, 128), jnp.float32),
            pltpu.VMEM((8, 2, 128), jnp.float32),
            dma((32,)), dma((32,)), dma((2, 3)), dma((2, 3)), dma((32,)), dma((32,)),
            dma((32,)), dma((32,)), dma((8,)), dma((8,)), dma((8,)), dma((8,)),
            dma((32,)), dma((32,)),
        ],
        compiler_params=pltpu.CompilerParams(collective_id=0, has_side_effects=True),
        name="exchange",
    )(masked, points, leafc, midc, ptop, geo, tgeo)
    table = node_table()
    trow = np.zeros((8, 128), np.float32)
    trow[:3] = np.tile(table, (1, 4))
    tcol = np.broadcast_to(table[:, :, None], (3, 32, 128)).astype(np.float32)
    return pl.pallas_call(
        down_kernel,
        out_shape=f32(16, 2048),
        in_specs=[SM] * 9 + [VM] * 13,
        out_specs=VM,
        scratch_shapes=[
            pltpu.VMEM((48, 32, 128), jnp.bfloat16),
            pltpu.VMEM((48, 8, 128), jnp.float32),
            pltpu.VMEM((12, 16, 128), jnp.float32),
            pltpu.VMEM((8, 16, 32), jnp.float32),
            pltpu.VMEM((3, 128, 128), jnp.float32),
            pltpu.VMEM((16, 16, 128), jnp.float32),
        ],
        name="down",
    )(
        counts, leaf_middle_owner, mid_parent, leaf_partners, mid_peers, mid_slots, top_offsets,
        geos.reshape(32, 128), tgeos.reshape(8, 128),
        masked, points, leafc, mhalo, phalo, lhalo, mids.reshape(64, 16, 128),
        tops.reshape(32, 16, 128), basis_t, leaf_basis_transfer, mid_transfer,
        jnp.asarray(trow), jnp.asarray(tcol),
    )


def solution(mesh):
    both = ("group", "leaf")
    placed = (
        P(None, both), P(None, both), P(both), P(both, None, None), P(both, None), P(both, None),
        P(both, None), P(both, None, None), P(both, None), P("group", "leaf"), P(both, None, None),
        P(both, None), P(both, None), P("group", None), P("group", None),
    )
    return jax.shard_map(
        on_device, mesh=mesh, in_specs=placed, out_specs=P(None, both), check_vma=False
    )
```

```python
import functools

import jax
import jax.numpy as jnp
import numpy as np
from jax import lax
from jax.experimental import pallas as pl
from jax.experimental.pallas import tpu as pltpu
from jax.sharding import PartitionSpec as P

MESH = pl.DeviceIdType.MESH
HI = lax.Precision.HIGHEST
PTS = 128
RANK = 32
RHS = 16
RATE = 1.7320508075688772 / 0.5
NX = 4
NZ = 8
NL = 32
NG = 8


def node_table():
    k = np.arange(RANK)
    rows = [
        np.cos(np.pi * (((k * (2 * d + 3)) % RANK) + 0.5) / RANK) for d in range(3)
    ]
    return np.stack(rows).astype(np.float32)


def nt(a, b, precision=HI):
    return lax.dot_general(
        a,
        b,
        (((1,), (1,)), ((), ())),
        precision=precision,
        preferred_element_type=jnp.float32,
    )


def nn(a, b):
    return lax.dot_general(
        a,
        b,
        (((1,), (0,)), ((), ())),
        precision=HI,
        preferred_element_type=jnp.float32,
    )


def kappa(squared):
    squared = jnp.maximum(squared, 1e-30)
    t = squared * lax.rsqrt(squared)
    return (1.0 + t) * jnp.exp(-t)


def block_of(shape):
    return lax.broadcasted_iota(jnp.int32, shape, 1) >> 5


def loop(count, width, f):
    def step(i, c):
        for e in range(width):
            f(i * width + e)
        return c

    lax.fori_loop(0, count // width, step, 0)


def whole_kernel(
    counts, owner, parent, partners, peers, slots, offsets, mgeo, lgeo, ggeo,
    points, rhs, basis_h, leaf_h, mid_h, trow, tcol,
    out,
    rhs_s, basis, leaf_t, mid_t, mwin, pwin, lwin, midc, ptop, geo, tgeo,
    mids, geos, tgeos, tops, rsbuf, zbuf, ztile,
    mhl, awin, bwin, base_s, far_m, p_s, w_s, mid_s, geos_v, tgeos_v,
    s_in, s_rs, r_rs, s_h, r_h, s_mid, r_mid, s_geo, r_geo, s_tg, r_tg, s_z, r_z, s_top, r_top,
):
    g = lax.axis_index("group")
    d = lax.axis_index("leaf")
    z = d // NX
    x = d % NX

    def leaf_peer(k):
        return (g, lax.rem(d + k, NL))

    def ring_peer(k):
        return (g, lax.rem(z + k, NZ) * NX + x)

    def plane_peer(k):
        return (lax.rem(g + k // NX, NG), z * NX + lax.rem(x + k % NX, NX))

    def each(lo, hi, f):
        def step(k, c):
            f(k)
            return c

        lax.fori_loop(lo, hi, step, 0)

    barrier = pltpu.get_barrier_semaphore()

    def hello(peer):
        pl.semaphore_signal(barrier, inc=1, device_id=peer, device_id_type=MESH)

    each(1, NL, lambda k: hello(leaf_peer(k)))
    each(1, 32, lambda k: hello(plane_peer(k)))

    loads = [
        pltpu.make_async_copy(a, b, s_in.at[i])
        for i, (a, b) in enumerate(
            [(rhs, rhs_s), (basis_h, basis), (leaf_h, leaf_t), (mid_h, mid_t), (points, pwin.at[1])]
        )
    ]
    for c in loads:
        c.start()

    def copy(src, dst, ss, rs, peer):
        return pltpu.make_async_remote_copy(
            src_ref=src, dst_ref=dst, send_sem=ss, recv_sem=rs, device_id=peer, device_id_type=MESH
        )

    def rs_copy(k):
        o = lax.rem(d + k, NL)
        return copy(
            ptop.at[(o % NX) * 8 + o // NX], rsbuf.at[k], s_rs.at[k], r_rs.at[k], leaf_peer(k)
        )

    def geo_copy(k):
        return copy(geo, geos_v.at[d], s_geo.at[k], r_geo.at[k], leaf_peer(k))

    def mid_copy(k):
        return copy(midc, mids.at[pl.ds(d * 2, 2)], s_mid.at[k], r_mid.at[k], leaf_peer(k))

    def tg_copy(k):
        return copy(tgeo, tgeos_v.at[g], s_tg.at[k], r_tg.at[k], (lax.rem(g + k, NG), d))

    def z_copy(k):
        return copy(zbuf.at[z], zbuf.at[z], s_z.at[k], r_z.at[k], ring_peer(k))

    def top_copy(k):
        return copy(ztile, tops.at[g * NX + x], s_top.at[k], r_top.at[k], plane_peer(k))

    lhalo, phalo = [], []
    for side in range(2):
        peer = leaf_peer(NL - 1 if side == 0 else 1)
        slot = 1 - side
        lhalo.append(
            copy(lwin.at[4:8], lwin.at[0:4] if side == 1 else lwin.at[8:12],
                 s_h.at[slot, 2], r_h.at[slot, 2], peer)
        )
        part = 0 if side == 1 else 2
        phalo.append(copy(pwin.at[1], pwin.at[part], s_h.at[slot, 0], r_h.at[slot, 0], peer))
        phalo.append(copy(mwin.at[1], mwin.at[part], s_h.at[slot, 1], r_h.at[slot, 1], peer))

    lane1 = lax.broadcasted_iota(jnp.int32, (1, 128), 1)
    row = jnp.zeros((1, 128), jnp.float32)
    for c in range(4):
        for i in range(8):
            row = jnp.where(lane1 == c * 8 + i, mgeo[c, i], row)
        for i in range(16):
            row = jnp.where(lane1 == 32 + c * 16 + i, lgeo[c, i], row)
    geo[...] = row
    geos_v[d] = row
    row = jnp.zeros((1, 128), jnp.float32)
    for c in range(4):
        for i in range(16):
            row = jnp.where(lane1 == c * 16 + i, ggeo[c, i], row)
    tgeo[...] = row
    tgeos_v[g] = row

    lane = lax.broadcasted_iota(jnp.int32, (RHS, PTS), 1)
    loads[0].wait()
    loads[1].wait()
    pieces = []
    for l in range(16):
        cols = slice(l * PTS, (l + 1) * PTS)
        m = jnp.where(lane < counts[l], rhs_s[:, cols], 0.0)
        mwin[1, :, cols] = m
        pieces.append(nt(m, basis[l]))
    loads[2].wait()
    loads[3].wait()
    loads[4].wait()
    srow = lax.broadcasted_iota(jnp.int32, (128, 128), 0) >> 4
    blk = block_of((128, 128))
    total = jnp.zeros((128, RANK), jnp.float32)
    for q in range(4):
        tile = jnp.concatenate(pieces[4 * q : 4 * q + 4], axis=1)
        lwin[4 + q] = tile
        own = jnp.full((128, 128), owner[0, 4 * q], jnp.int32)
        for b in range(1, 4):
            own = jnp.where(blk == b, owner[0, 4 * q + b], own)
        lhs = jnp.where(own == srow, jnp.concatenate([tile] * 8, axis=0), 0.0)
        total = total + nn(lhs, leaf_t[4 * q : 4 * q + 4].reshape(128, RANK))
    srow = lax.broadcasted_iota(jnp.int32, (256, 128), 0) >> 4
    blk = block_of((256, 128))
    topp = jnp.zeros((256, RANK), jnp.float32)
    for q in range(2):
        tile = jnp.concatenate(
            [total[(4 * q + b) * 16 : (4 * q + b + 1) * 16] for b in range(4)], axis=1
        )
        midc[q] = tile
        own = jnp.full((256, 128), parent[0, 4 * q], jnp.int32)
        for b in range(1, 4):
            own = jnp.where(blk == b, parent[0, 4 * q + b], own)
        lhs = jnp.where(own == srow, jnp.concatenate([tile] * 16, axis=0), 0.0)
        topp = topp + nn(lhs, mid_t[4 * q : 4 * q + 4].reshape(128, RANK))
    for q in range(4):
        tile = jnp.concatenate(
            [topp[(4 * q + b) * 16 : (4 * q + b + 1) * 16] for b in range(4)], axis=1
        )
        for i in range(8):
            ptop[q * 8 + i] = tile[2 * i : 2 * i + 2]

    pl.semaphore_wait(barrier, 62)
    each(1, NL, lambda k: rs_copy(k).start())
    for c in phalo:
        c.start()
    each(1, NL, lambda k: geo_copy(k).start())
    each(1, NG, lambda k: tg_copy(k).start())
    for c in lhalo:
        c.start()

    def make_w(l):
        w_s[l] = lax.dot_general(
            leaf_t[l], basis[l], (((0,), (0,)), ((), ())), precision=HI,
            preferred_element_type=jnp.float32,
        )

    loop(16, 4, make_w)

    sub = lax.broadcasted_iota(jnp.int32, (8, PTS), 0)

    def split3(v):
        a = v.astype(jnp.bfloat16).astype(jnp.float32)
        r = v - a
        b = r.astype(jnp.bfloat16).astype(jnp.float32)
        return a, b, r - b

    def window(part, i):
        cols = pl.ds(pl.multiple_of(i * PTS, PTS), PTS)
        m = mwin[part, :, cols]
        high = m.astype(jnp.bfloat16)
        low = (m - high.astype(jnp.float32)).astype(jnp.bfloat16)
        w = part * 16 + i
        mhl[w] = jnp.concatenate([high, low], axis=0)
        c = (pwin[part, :, cols] - 0.5) * RATE
        norm = jnp.sum(c * c, axis=0, keepdims=True)
        c8 = jnp.concatenate([c, jnp.zeros((5, PTS), jnp.float32)], axis=0)
        v = jnp.where(sub == 3, norm, jnp.where(sub == 4, 1.0, c8))
        a, b, e = split3(v)
        bwin[w] = jnp.concatenate([a, a, a, b, b, e], axis=0).astype(jnp.bfloat16)
        if part == 1:
            v = jnp.where(sub == 3, 1.0, jnp.where(sub == 4, norm, -2.0 * c8))
            a, b, e = split3(v)
            awin[i] = jnp.concatenate([a, b, e, a, b, a], axis=0).T.astype(jnp.bfloat16)

    loop(16, 2, lambda i: window(1, i))

    def near(l):
        target = awin[l]
        both = jnp.zeros((PTS, 2 * RHS), jnp.float32)
        rest = jnp.zeros((PTS, RHS), jnp.float32)
        for j in range(0, 8, 2):
            ws = [l + 16 + partners[l, j + e] for e in range(2)]
            source = jnp.concatenate([bwin[w] for w in ws], axis=1)
            k = kappa(
                lax.dot_general(
                    target, source, (((1,), (0,)), ((), ())), preferred_element_type=jnp.float32
                )
            )
            high = k.astype(jnp.bfloat16)
            low = (k - high.astype(jnp.float32)).astype(jnp.bfloat16)
            m = jnp.concatenate([mhl[w] for w in ws], axis=1)
            both = both + nt(high, m, None)
            rest = rest + nt(low, m[:RHS], None)
        base_s[l] = (both[:, :RHS] + both[:, RHS:] + rest).T

    def near_range(lo, hi):
        each(lo, hi, near)

    for c in phalo:
        c.wait_recv()
    loop(16, 2, lambda i: window(0, i))
    loop(16, 2, lambda i: window(2, i))
    near_range(0, N1)

    each(1, NL, lambda k: rs_copy(k).wait_recv())
    total = ptop[x * 8 + z]
    for k in range(1, NL):
        total = total + rsbuf[k]
    zbuf[z] = total
    each(1, NZ, lambda k: z_copy(k).start())
    each(1, NL, lambda k: mid_copy(k).start())
    mids[pl.ds(d * 2, 2)] = midc[...]
    near_range(N1, N2)
    each(1, NZ, lambda k: z_copy(k).wait_recv())
    for i in range(8):
        ztile[2 * i : 2 * i + 2] = zbuf[i]
    each(1, 32, lambda k: top_copy(k).start())
    tops[g * NX + x] = ztile[...]
    near_range(N2, 16)

    each(1, NL, lambda k: geo_copy(k).wait_recv())
    each(1, NG, lambda k: tg_copy(k).wait_recv())
    for c in lhalo:
        c.wait_recv()
    to_smem = [
        pltpu.make_async_copy(geos_v, geos, s_in.at[0]),
        pltpu.make_async_copy(tgeos_v, tgeos, s_in.at[1]),
    ]
    for c in to_smem:
        c.start()
    for c in to_smem:
        c.wait()

    blk16 = block_of((RHS, 128))
    blk1 = block_of((1, 128))

    def gather(tab, srcs):
        acc = None
        for j, s in enumerate(srcs):
            t = pltpu.roll(tab[s >> 2], ((j - (s & 3)) & 3) * 32, 1)
            acc = t if j == 0 else jnp.where(blk16 == j, t, acc)
        return acc

    def target_nodes(read):
        h = read(3)
        return [(read(c) + h * tcol[c]) * RATE for c in range(3)]

    def coupling(tnodes, reads):
        def mix(c):
            v = jnp.full((1, 128), reads[0](c), jnp.float32)
            for j in range(1, 4):
                v = jnp.where(blk1 == j, reads[j](c), v)
            return v

        h = mix(3)
        squared = None
        for c in range(3):
            r = (mix(c) + h * trow[c : c + 1, :]) * RATE
            diff = tnodes[c] - r
            squared = diff * diff if squared is None else squared + diff * diff
        return kappa(squared)

    def top_read(s):
        return lambda c: tgeos[s >> 4, 0, c * 16 + (s & 15)]

    def mid_read(i):
        return lambda c: geos[i >> 3, 0, c * 8 + (i & 7)]

    def leaf_read(w):
        dev = lax.rem(d + NL - 1 + (w >> 4), NL)
        return lambda c: geos[dev, 0, 32 + c * 16 + (w & 15)]

    def leaf_far(l):
        nodes = target_nodes(leaf_read(l + 16))
        cs, ss = [], []
        for q in range(2):
            srcs = [l + 16 + partners[l, 8 + 4 * q + j] for j in range(4)]
            cs.append(gather(lwin, srcs))
            ss.append(coupling(nodes, [leaf_read(s) for s in srcs]))
        local = nt(jnp.concatenate(cs, axis=1), jnp.concatenate(ss, axis=1))
        base_s[l] += nn(local, basis[l])

    loop(16, 2, leaf_far)

    def top_sources(b):
        p = parent[0, b]
        t = g * 16 + p
        return t, [[(t + offsets[p, 4 * q + j]) & 127 for j in range(4)] for q in range(4)]

    def top_coupling(b):
        t, srcs = top_sources(b)
        nodes = target_nodes(top_read(t))
        s = [coupling(nodes, [top_read(i) for i in four]) for four in srcs]
        p_s[b] = nn(mid_t[b], jnp.concatenate(s, axis=1))

    loop(8, 2, top_coupling)

    each(1, NL, lambda k: mid_copy(k).wait_recv())

    def mid_coupling(b):
        nodes = target_nodes(mid_read(d * 8 + b))
        cs, ss = [], []
        for q in range(2):
            srcs = [peers[b, 4 * q + j] * 8 + slots[b, 4 * q + j] for j in range(4)]
            cs.append(gather(mids, srcs))
            ss.append(coupling(nodes, [mid_read(s) for s in srcs]))
        far_m[b] = nt(jnp.concatenate(cs, axis=1), jnp.concatenate(ss, axis=1))

    loop(8, 2, mid_coupling)

    each(1, 32, lambda k: top_copy(k).wait_recv())

    def down_mid(b):
        _, srcs = top_sources(b)
        c = jnp.concatenate([gather(tops, four) for four in srcs], axis=1)
        mid_s[b] = far_m[b] + nt(c, p_s[b])

    loop(8, 4, down_mid)

    for l in range(16):
        cols = slice(l * PTS, (l + 1) * PTS)
        value = base_s[l] + nn(mid_s[owner[0, l]], w_s[l])
        out[:, cols] = jnp.where(lane < counts[l], value, 0.0)

    each(1, NL, lambda k: rs_copy(k).wait_send())
    each(1, NL, lambda k: geo_copy(k).wait_send())
    each(1, NG, lambda k: tg_copy(k).wait_send())
    each(1, NZ, lambda k: z_copy(k).wait_send())
    each(1, NL, lambda k: mid_copy(k).wait_send())
    each(1, 32, lambda k: top_copy(k).wait_send())
    for c in lhalo + phalo:
        c.wait_send()


N1 = 3
N2 = 9
VM = pl.BlockSpec(memory_space=pltpu.VMEM)
SM = pl.BlockSpec(memory_space=pltpu.SMEM)
ANY = pl.BlockSpec(memory_space=pl.ANY)


def on_device(
    points, rhs, counts, basis, leaf_geom, leaf_partners, leaf_middle_owner, leaf_basis_transfer,
    mid_geom, mid_parent, mid_transfer, mid_peers, mid_slots, top_geom, top_offsets,
):
    table = node_table()
    trow = np.zeros((8, 128), np.float32)
    trow[:3] = np.tile(table, (1, 4))
    tcol = np.broadcast_to(table[:, :, None], (3, 32, 128)).astype(np.float32)
    dma = pltpu.SemaphoreType.DMA

    def vm(*shape, dtype=jnp.float32):
        return pltpu.VMEM(shape, dtype)

    return pl.pallas_call(
        whole_kernel,
        out_shape=jax.ShapeDtypeStruct((16, 2048), jnp.float32),
        in_specs=[SM] * 10 + [ANY] * 5 + [VM] * 2,
        out_specs=VM,
        scratch_shapes=[
            vm(16, 2048), vm(16, 32, 128), vm(16, 32, 32), vm(8, 32, 32),
            vm(3, 16, 2048), vm(3, 3, 2048), vm(12, 16, 128), vm(2, 16, 128), vm(32, 2, 128),
            vm(1, 128), vm(1, 128),
            vm(64, 16, 128), pltpu.SMEM((32, 1, 128), jnp.float32),
            pltpu.SMEM((8, 1, 128), jnp.float32), vm(32, 16, 128),
            vm(32, 2, 128), vm(8, 2, 128), vm(16, 128),
            vm(48, 32, 128, dtype=jnp.bfloat16), vm(16, 128, 48, dtype=jnp.bfloat16),
            vm(48, 48, 128, dtype=jnp.bfloat16),
            vm(16, 16, 128), vm(8, 16, 32), vm(8, 32, 512), vm(16, 32, 128), vm(8, 16, 32),
            vm(32, 1, 128), vm(8, 1, 128),
            dma((5,)),
            dma((32,)), dma((32,)), dma((2, 3)), dma((2, 3)), dma((32,)), dma((32,)),
            dma((32,)), dma((32,)), dma((8,)), dma((8,)), dma((8,)), dma((8,)),
            dma((32,)), dma((32,)),
        ],
        compiler_params=pltpu.CompilerParams(collective_id=0, has_side_effects=True),
        name="whole",
    )(
        counts, leaf_middle_owner, mid_parent, leaf_partners, mid_peers, mid_slots, top_offsets,
        mid_geom.T, leaf_geom.T, top_geom.T,
        points, rhs, jnp.swapaxes(basis, 1, 2), leaf_basis_transfer, mid_transfer,
        jnp.asarray(trow), jnp.asarray(tcol),
    )


def solution(mesh):
    both = ("group", "leaf")
    placed = (
        P(None, both), P(None, both), P(both), P(both, None, None), P(both, None), P(both, None),
        P(both, None), P(both, None, None), P(both, None), P("group", "leaf"), P(both, None, None),
        P(both, None), P(both, None), P("group", None), P("group", None),
    )
    return jax.shard_map(
        on_device, mesh=mesh, in_specs=placed, out_specs=P(None, both), check_vma=False
    )
```

```python
import functools

import jax
import jax.numpy as jnp
import numpy as np
from jax import lax
from jax.experimental import pallas as pl
from jax.experimental.pallas import tpu as pltpu
from jax.sharding import PartitionSpec as P

MESH = pl.DeviceIdType.MESH
PTS = 128
RANK = 32
RHS = 16
RATE = 1.7320508075688772 / 0.5
NX = 4
NZ = 8
NL = 32
NG = 8


def node_table():
    k = np.arange(RANK)
    rows = [
        np.cos(np.pi * (((k * (2 * d + 3)) % RANK) + 0.5) / RANK) for d in range(3)
    ]
    return np.stack(rows).astype(np.float32)


def bf(a):
    return a.astype(jnp.bfloat16)


def raw(a, b, ca, cb):
    return lax.dot_general(
        a, b, (((ca,), (cb,)), ((), ())), preferred_element_type=jnp.float32
    )


def dot3(a, b, ca, cb):
    ah, bh = bf(a), bf(b)
    al, bl = bf(a - ah.astype(jnp.float32)), bf(b - bh.astype(jnp.float32))
    return raw(ah, bh, ca, cb) + (raw(al, bh, ca, cb) + raw(ah, bl, ca, cb))


def nt(a, b):
    return dot3(a, b, 1, 1)


def nn(a, b):
    return dot3(a, b, 1, 0)


def kappa(squared):
    squared = jnp.maximum(squared, 1e-30)
    t = squared * lax.rsqrt(squared)
    return (1.0 + t) * jnp.exp(-t)


def block_of(shape):
    return lax.broadcasted_iota(jnp.int32, shape, 1) >> 5


def loop(count, width, f):
    def step(i, c):
        for e in range(width):
            f(i * width + e)
        return c

    lax.fori_loop(0, count // width, step, 0)


def mask_kernel(counts, product, out):
    lane = lax.broadcasted_iota(jnp.int32, (RHS, PTS), 1)
    for l in range(16):
        cols = slice(l * PTS, (l + 1) * PTS)
        out[:, cols] = jnp.where(lane < counts[l], product[:, cols], 0.0)


def whole_kernel(
    counts_h, owner_h, parent_h, partners_h, peers_h, slots_h, offsets_h, mgeo_h, lgeo_h, ggeo_h,
    points, rhs, basis_h, leaf_h, mid_h, trow_h, tcol_h,
    out,
    counts, owner, parent, partners, peers, slots, offsets, mgeo, lgeo, ggeo, trow, tcol,
    rhs_s, basis, leaf_t, mid_t, mwin, pwin, lwin, midc, ptop, geo, tgeo,
    mids, geos, tgeos, tops, rsbuf, zbuf, ztile,
    mhl, pts, tb, kb0, kb1, base_s, far_m, p_s, w_s, mid_s, geos_v, tgeos_v,
    s_in, sends, recvs,
):
    g = lax.axis_index("group")
    d = lax.axis_index("leaf")
    z = d // NX
    x = d % NX

    def leaf_peer(a, b):
        return (g, lax.rem(z + a, NZ) * NX + lax.rem(x + b, NX))

    def plane_peer(a, b):
        return (lax.rem(g + a, NG), z * NX + lax.rem(x + b, NX))

    def each(lo, hi, f):
        def step(k, c):
            f(k)
            return c

        lax.fori_loop(lo, hi, step, 0)

    def others(count, f):
        for b in range(1, NX):
            f(0, b)

        def rest(a):
            for b in range(NX):
                f(a, b)

        each(1, count, rest)

    barrier = pltpu.get_barrier_semaphore()

    def hello(peer):
        pl.semaphore_signal(barrier, inc=1, device_id=peer, device_id_type=MESH)

    others(NZ, lambda a, b: hello(leaf_peer(a, b)))
    others(NG, lambda a, b: hello(plane_peer(a, b)))

    loads = [
        pltpu.make_async_copy(a, b, s_in.at[i])
        for i, (a, b) in enumerate(
            [
                (counts_h, counts), (rhs, rhs_s), (basis_h, basis), (owner_h, owner),
                (parent_h, parent), (leaf_h, leaf_t), (mid_h, mid_t), (points, pwin.at[1]),
                (mgeo_h, mgeo), (lgeo_h, lgeo), (ggeo_h, ggeo),
                (partners_h, partners), (peers_h, peers), (slots_h, slots),
                (offsets_h, offsets), (trow_h, trow), (tcol_h, tcol),
            ]
        )
    ]
    for c in loads:
        c.start()

    def copy(src, dst, ss, rs, peer):
        return pltpu.make_async_remote_copy(
            src_ref=src, dst_ref=dst, send_sem=ss, recv_sem=rs, device_id=peer, device_id_type=MESH
        )

    def rs_copy(a, b):
        piece = ptop.at[lax.rem(x + b, NX) * NZ + lax.rem(z + a, NZ)]
        return copy(piece, rsbuf.at[a * NX + b], sends.at[0], recvs.at[0], leaf_peer(a, b))

    def geo_copy(a, b):
        return copy(geo, geos_v.at[d], sends.at[1], recvs.at[1], leaf_peer(a, b))

    def mid_copy(a, b):
        return copy(midc, mids.at[pl.ds(d * 2, 2)], sends.at[2], recvs.at[2], leaf_peer(a, b))

    def tg_copy(k):
        return copy(tgeo, tgeos_v.at[g], sends.at[3], recvs.at[3], (lax.rem(g + k, NG), d))

    def z_copy(k):
        return copy(zbuf.at[z], zbuf.at[z], sends.at[4], recvs.at[4], leaf_peer(k, 0))

    def top_copy(a, b):
        return copy(ztile, tops.at[g * NX + x], sends.at[5], recvs.at[5], plane_peer(a, b))

    whole = [
        rsbuf.at[pl.ds(1, NL - 1)], geos_v.at[pl.ds(0, NL - 1)], mids.at[pl.ds(0, 2 * NL - 2)],
        tgeos_v.at[pl.ds(0, NG - 1)], zbuf.at[pl.ds(0, NZ - 1)], tops.at[pl.ds(0, 31)],
        pwin.at[pl.ds(0, 2)], mwin.at[pl.ds(0, 2)], lwin.at[pl.ds(0, 8)],
    ]

    def got(i):
        pltpu.make_async_copy(whole[i], whole[i], recvs.at[i]).wait()

    def sent(i):
        pltpu.make_async_copy(whole[i], whole[i], sends.at[i]).wait()

    lhalo, phalo = [], []
    for side in range(2):
        part = 2 - 2 * side
        peer = (g, lax.rem(d + (NL - 1 if side == 0 else 1), NL))
        lhalo.append(
            copy(lwin.at[4:8], lwin.at[4 * part : 4 * part + 4], sends.at[8], recvs.at[8], peer)
        )
        phalo.append(copy(pwin.at[1], pwin.at[part], sends.at[6], recvs.at[6], peer))
        phalo.append(copy(mwin.at[1], mwin.at[part], sends.at[7], recvs.at[7], peer))

    lane = lax.broadcasted_iota(jnp.int32, (RHS, PTS), 1)
    for i in range(3):
        loads[i].wait()
    pieces = []
    for l in range(16):
        cols = slice(l * PTS, (l + 1) * PTS)
        m = jnp.where(lane < counts[l], rhs_s[:, cols], 0.0)
        mwin[1, :, cols] = m
        pieces.append(nt(m, basis[l]))
    for i in range(3, 8):
        loads[i].wait()
    srow = lax.broadcasted_iota(jnp.int32, (128, 128), 0) >> 4
    blk = block_of((128, 128))
    total = jnp.zeros((128, RANK), jnp.float32)
    for q in range(4):
        tile = jnp.concatenate(pieces[4 * q : 4 * q + 4], axis=1)
        lwin[4 + q] = tile
        own = jnp.full((128, 128), owner[0, 4 * q], jnp.int32)
        for b in range(1, 4):
            own = jnp.where(blk == b, owner[0, 4 * q + b], own)
        lhs = jnp.where(own == srow, jnp.concatenate([tile] * 8, axis=0), 0.0)
        total = total + nn(lhs, leaf_t[4 * q : 4 * q + 4].reshape(128, RANK))
    srow = lax.broadcasted_iota(jnp.int32, (256, 128), 0) >> 4
    blk = block_of((256, 128))
    topp = jnp.zeros((256, RANK), jnp.float32)
    for q in range(2):
        tile = jnp.concatenate(
            [total[(4 * q + b) * 16 : (4 * q + b + 1) * 16] for b in range(4)], axis=1
        )
        midc[q] = tile
        own = jnp.full((256, 128), parent[0, 4 * q], jnp.int32)
        for b in range(1, 4):
            own = jnp.where(blk == b, parent[0, 4 * q + b], own)
        lhs = jnp.where(own == srow, jnp.concatenate([tile] * 16, axis=0), 0.0)
        topp = topp + nn(lhs, mid_t[4 * q : 4 * q + 4].reshape(128, RANK))
    for q in range(4):
        tile = jnp.concatenate(
            [topp[(4 * q + b) * 16 : (4 * q + b + 1) * 16] for b in range(4)], axis=1
        )
        for i in range(8):
            ptop[q * 8 + i] = tile[2 * i : 2 * i + 2]

    for i in range(8, 17):
        loads[i].wait()
    lane1 = lax.broadcasted_iota(jnp.int32, (1, 128), 1)
    row = jnp.zeros((1, 128), jnp.float32)
    for c in range(4):
        for i in range(8):
            row = jnp.where(lane1 == c * 8 + i, mgeo[c, i], row)
        for i in range(16):
            row = jnp.where(lane1 == 32 + c * 16 + i, lgeo[c, i], row)
    geo[...] = row
    geos_v[d] = row
    row = jnp.zeros((1, 128), jnp.float32)
    for c in range(4):
        for i in range(16):
            row = jnp.where(lane1 == c * 16 + i, ggeo[c, i], row)
    tgeo[...] = row
    tgeos_v[g] = row

    pl.semaphore_wait(barrier, 62)
    others(NZ, lambda a, b: rs_copy(a, b).start())
    for c in phalo:
        c.start()
    others(NZ, lambda a, b: geo_copy(a, b).start())
    each(1, NG, lambda k: tg_copy(k).start())
    for c in lhalo:
        c.start()

    def make_w(l):
        w_s[l] = dot3(leaf_t[l], basis[l], 0, 0)

    loop(16, 4, make_w)

    def window(part, i):
        cols = pl.ds(pl.multiple_of(i * PTS, PTS), PTS)
        m = mwin[part, :, cols]
        high = bf(m)
        w = part * 16 + i
        mhl[w] = jnp.concatenate([high, bf(m - high.astype(jnp.float32))], axis=0)
        c = pwin[part, :, cols] * RATE
        pts[w] = jnp.concatenate([c, jnp.zeros((5, PTS), jnp.float32)], axis=0)

    loop(16, 4, lambda i: window(1, i))

    def distances(l, kb):
        target = pts[l + 16].T
        for c in range(3):
            tb[c] = jnp.broadcast_to(target[:, c : c + 1], (PTS, PTS))
        for j in range(8):
            w = l + 16 + partners[l, j]
            squared = None
            for c in range(3):
                diff = tb[c] - pts[w, c : c + 1, :]
                squared = diff * diff if squared is None else squared + diff * diff
            k = kappa(squared)
            high = bf(k)
            cols = slice((j % 2) * PTS, (j % 2 + 1) * PTS)
            kb[j // 2, 0:PTS, cols] = high
            kb[j // 2, PTS : 2 * PTS, cols] = bf(k - high.astype(jnp.float32))

    def products(l, kb):
        acc = jnp.zeros((2 * RHS, 2 * PTS), jnp.float32)
        for j in range(4):
            ws = [l + 16 + partners[l, 2 * j + e] for e in range(2)]
            m = jnp.concatenate([mhl[w] for w in ws], axis=1)
            acc = acc + raw(m, kb[j], 1, 1)
        base_s[l] = acc[:RHS, :PTS] + (acc[RHS:, :PTS] + acc[:RHS, PTS:])

    def near(i):
        distances(2 * i + 1, kb1)
        products(2 * i, kb0)
        distances(jnp.minimum(2 * i + 2, 15), kb0)
        products(2 * i + 1, kb1)

    got(6)
    got(7)
    loop(16, 4, lambda i: window(0, i))
    loop(16, 4, lambda i: window(2, i))
    distances(0, kb0)
    each(0, N1, near)

    got(0)
    terms = [ptop[x * 8 + z]] + [rsbuf[k] for k in range(1, NL)]
    while len(terms) > 1:
        terms = [a + b for a, b in zip(terms[::2], terms[1::2])]
    zbuf[z] = terms[0]
    each(1, NZ, lambda k: z_copy(k).start())
    others(NZ, lambda a, b: mid_copy(a, b).start())
    mids[pl.ds(d * 2, 2)] = midc[...]
    each(N1, N2, near)
    got(4)
    for i in range(8):
        ztile[2 * i : 2 * i + 2] = zbuf[i]
    others(NG, lambda a, b: top_copy(a, b).start())
    tops[g * NX + x] = ztile[...]
    each(N2, 8, near)

    got(1)
    got(3)
    got(8)
    to_smem = [
        pltpu.make_async_copy(geos_v, geos, s_in.at[0]),
        pltpu.make_async_copy(tgeos_v, tgeos, s_in.at[1]),
    ]
    for c in to_smem:
        c.start()
    for c in to_smem:
        c.wait()

    blk16 = block_of((RHS, 128))
    blk1 = block_of((1, 128))

    def gather(tab, srcs):
        acc = None
        for j, s in enumerate(srcs):
            t = pltpu.roll(tab[s >> 2], ((j - (s & 3)) & 3) * 32, 1)
            acc = t if j == 0 else jnp.where(blk16 == j, t, acc)
        return acc

    def target_nodes(read):
        h = read(3)
        return [(read(c) + h * tcol[c]) * RATE for c in range(3)]

    def coupling(tnodes, reads):
        def mix(c):
            v = jnp.full((1, 128), reads[0](c), jnp.float32)
            for j in range(1, 4):
                v = jnp.where(blk1 == j, reads[j](c), v)
            return v

        h = mix(3)
        squared = None
        for c in range(3):
            r = (mix(c) + h * trow[c : c + 1, :]) * RATE
            diff = tnodes[c] - r
            squared = diff * diff if squared is None else squared + diff * diff
        return kappa(squared)

    def top_read(s):
        return lambda c: tgeos[s >> 4, 0, c * 16 + (s & 15)]

    def mid_read(i):
        return lambda c: geos[i >> 3, 0, c * 8 + (i & 7)]

    def leaf_read(w):
        dev = lax.rem(d + NL - 1 + (w >> 4), NL)
        return lambda c: geos[dev, 0, 32 + c * 16 + (w & 15)]

    def leaf_far(l):
        nodes = target_nodes(leaf_read(l + 16))
        cs, ss = [], []
        for q in range(2):
            srcs = [l + 16 + partners[l, 8 + 4 * q + j] for j in range(4)]
            cs.append(gather(lwin, srcs))
            ss.append(coupling(nodes, [leaf_read(s) for s in srcs]))
        local = nt(jnp.concatenate(cs, axis=1), jnp.concatenate(ss, axis=1))
        base_s[l] += nn(local, basis[l])

    loop(16, 2, leaf_far)

    def top_sources(b):
        p = parent[0, b]
        t = g * 16 + p
        return t, [[(t + offsets[p, 4 * q + j]) & 127 for j in range(4)] for q in range(4)]

    def top_coupling(b):
        t, srcs = top_sources(b)
        nodes = target_nodes(top_read(t))
        s = [coupling(nodes, [top_read(i) for i in four]) for four in srcs]
        p_s[b] = nn(mid_t[b], jnp.concatenate(s, axis=1))

    loop(8, 2, top_coupling)

    got(2)

    def mid_coupling(b):
        nodes = target_nodes(mid_read(d * 8 + b))
        cs, ss = [], []
        for q in range(2):
            srcs = [peers[b, 4 * q + j] * 8 + slots[b, 4 * q + j] for j in range(4)]
            cs.append(gather(mids, srcs))
            ss.append(coupling(nodes, [mid_read(s) for s in srcs]))
        far_m[b] = nt(jnp.concatenate(cs, axis=1), jnp.concatenate(ss, axis=1))

    loop(8, 2, mid_coupling)

    got(5)

    def down_mid(b):
        _, srcs = top_sources(b)
        c = jnp.concatenate([gather(tops, four) for four in srcs], axis=1)
        mid_s[b] = far_m[b] + nt(c, p_s[b])

    loop(8, 4, down_mid)

    for l in range(16):
        cols = slice(l * PTS, (l + 1) * PTS)
        value = base_s[l] + nn(mid_s[owner[0, l]], w_s[l])
        out[:, cols] = value

    for i in range(9):
        sent(i)


N1 = 2
N2 = 4
VM = pl.BlockSpec(memory_space=pltpu.VMEM)
SM = pl.BlockSpec(memory_space=pltpu.SMEM)
ANY = pl.BlockSpec(memory_space=pl.ANY)


def on_device(
    points, rhs, counts, basis, leaf_geom, leaf_partners, leaf_middle_owner, leaf_basis_transfer,
    mid_geom, mid_parent, mid_transfer, mid_peers, mid_slots, top_geom, top_offsets,
):
    table = node_table()
    trow = np.zeros((8, 128), np.float32)
    trow[:3] = np.tile(table, (1, 4))
    tcol = np.broadcast_to(table[:, :, None], (3, 32, 128)).astype(np.float32)
    dma = pltpu.SemaphoreType.DMA

    def vm(*shape, dtype=jnp.float32):
        return pltpu.VMEM(shape, dtype)

    def sm(*shape, dtype=jnp.int32):
        return pltpu.SMEM(shape, dtype)

    product = pl.pallas_call(
        whole_kernel,
        out_shape=jax.ShapeDtypeStruct((16, 2048), jnp.float32),
        in_specs=[ANY] * 17,
        out_specs=VM,
        scratch_shapes=[
            sm(16), sm(1, 16), sm(1, 8), sm(16, 16), sm(8, 8), sm(8, 8), sm(16, 16),
            sm(4, 8, dtype=jnp.float32), sm(4, 16, dtype=jnp.float32),
            sm(4, 16, dtype=jnp.float32), vm(8, 128), vm(3, 32, 128),
            vm(16, 2048), vm(16, 32, 128), vm(16, 32, 32), vm(8, 32, 32),
            vm(3, 16, 2048), vm(3, 3, 2048), vm(12, 16, 128), vm(2, 16, 128), vm(32, 2, 128),
            vm(1, 128), vm(1, 128),
            vm(64, 16, 128), pltpu.SMEM((32, 1, 128), jnp.float32),
            pltpu.SMEM((8, 1, 128), jnp.float32), vm(32, 16, 128),
            vm(32, 2, 128), vm(8, 2, 128), vm(16, 128),
            vm(48, 32, 128, dtype=jnp.bfloat16), vm(48, 8, 128),
            vm(3, 128, 128), vm(4, 256, 256, dtype=jnp.bfloat16),
            vm(4, 256, 256, dtype=jnp.bfloat16),
            vm(16, 16, 128), vm(8, 16, 32), vm(8, 32, 512), vm(16, 32, 128), vm(8, 16, 32),
            vm(32, 1, 128), vm(8, 1, 128),
            dma((17,)), dma((9,)), dma((9,)),
        ],
        compiler_params=pltpu.CompilerParams(collective_id=0, has_side_effects=True),
        name="whole",
    )(
        counts, leaf_middle_owner, mid_parent, leaf_partners, mid_peers, mid_slots, top_offsets,
        mid_geom.T, leaf_geom.T, top_geom.T,
        points, rhs, jnp.swapaxes(basis, 1, 2), leaf_basis_transfer, mid_transfer,
        jnp.asarray(trow), jnp.asarray(tcol),
    )
    return pl.pallas_call(
        mask_kernel,
        out_shape=jax.ShapeDtypeStruct((16, 2048), jnp.float32),
        in_specs=[SM, VM],
        out_specs=VM,
        name="mask",
    )(counts, product)


def solution(mesh):
    both = ("group", "leaf")
    placed = (
        P(None, both), P(None, both), P(both), P(both, None, None), P(both, None), P(both, None),
        P(both, None), P(both, None, None), P(both, None), P("group", "leaf"), P(both, None, None),
        P(both, None), P(both, None), P("group", None), P("group", None),
    )
    return jax.shard_map(
        on_device, mesh=mesh, in_specs=placed, out_specs=P(None, both), check_vma=False
    )
```

```python
import functools

import jax
import jax.numpy as jnp
import numpy as np
from jax import lax
from jax.experimental import pallas as pl
from jax.experimental.pallas import tpu as pltpu
from jax.sharding import PartitionSpec as P

MESH = pl.DeviceIdType.MESH
PTS = 128
RANK = 32
RHS = 16
RATE = 1.7320508075688772 / 0.5
NX = 4
NZ = 8
NL = 32
NG = 8


def node_table():
    k = np.arange(RANK)
    rows = [
        np.cos(np.pi * (((k * (2 * d + 3)) % RANK) + 0.5) / RANK) for d in range(3)
    ]
    return np.stack(rows).astype(np.float32)


def bf(a):
    return a.astype(jnp.bfloat16)


def raw(a, b, ca, cb):
    return lax.dot_general(
        a, b, (((ca,), (cb,)), ((), ())), preferred_element_type=jnp.float32
    )


def dot3(a, b, ca, cb):
    ah, bh = bf(a), bf(b)
    al, bl = bf(a - ah.astype(jnp.float32)), bf(b - bh.astype(jnp.float32))
    return raw(ah, bh, ca, cb) + (raw(al, bh, ca, cb) + raw(ah, bl, ca, cb))


def nt(a, b):
    return dot3(a, b, 1, 1)


def nn(a, b):
    return dot3(a, b, 1, 0)


def kappa(squared):
    squared = jnp.maximum(squared, 1e-30)
    t = squared * lax.rsqrt(squared)
    return (1.0 + t) * jnp.exp2(t * -1.4426950408889634)


def block_of(shape):
    return lax.broadcasted_iota(jnp.int32, shape, 1) >> 5


def loop(count, width, f):
    def step(i, c):
        for e in range(width):
            f(i * width + e)
        return c

    lax.fori_loop(0, count // width, step, 0)


def mask_kernel(counts, product, out):
    lane = lax.broadcasted_iota(jnp.int32, (RHS, PTS), 1)
    for l in range(16):
        cols = slice(l * PTS, (l + 1) * PTS)
        out[:, cols] = jnp.where(lane < counts[l], product[:, cols], 0.0)


def whole_kernel(
    counts_h, owner_h, parent_h, partners_h, peers_h, slots_h, offsets_h, mgeo_h, lgeo_h, ggeo_h,
    points, rhs, basis_h, leaf_h, mid_h, trow_h, tcol_h,
    out,
    counts, owner, parent, partners, peers, slots, offsets, mgeo, lgeo, ggeo, trow, tcol,
    rhs_s, basis, leaf_t, mid_t, mwin, pwin, lwin, midc, ptop, geo, tgeo,
    mids, geos, tgeos, tops, rsbuf, zbuf, ztile,
    mhl, awin, bwin, sb0, sb1, kb0, kb1, base_s, far_l, far_m, p_s, w_s, mid_s, geos_v, tgeos_v,
    s_in, sends, recvs,
):
    g = lax.axis_index("group")
    d = lax.axis_index("leaf")
    z = d // NX
    x = d % NX

    def leaf_peer(a, b):
        return (g, lax.rem(z + a, NZ) * NX + lax.rem(x + b, NX))

    def plane_peer(a, b):
        return (lax.rem(g + a, NG), z * NX + lax.rem(x + b, NX))

    def each(lo, hi, f):
        def step(k, c):
            f(k)
            return c

        lax.fori_loop(lo, hi, step, 0)

    def others(count, f):
        for b in range(1, NX):
            f(0, b)

        def rest(a):
            for b in range(NX):
                f(a, b)

        each(1, count, rest)

    barrier = pltpu.get_barrier_semaphore()

    def hello(peer):
        pl.semaphore_signal(barrier, inc=1, device_id=peer, device_id_type=MESH)

    others(NZ, lambda a, b: hello(leaf_peer(a, b)))
    others(NG, lambda a, b: hello(plane_peer(a, b)))

    loads = [
        pltpu.make_async_copy(a, b, s_in.at[i])
        for i, (a, b) in enumerate(
            [
                (counts_h, counts), (rhs, rhs_s), (basis_h, basis), (owner_h, owner),
                (parent_h, parent), (leaf_h, leaf_t), (mid_h, mid_t), (points, pwin.at[1]),
                (mgeo_h, mgeo), (lgeo_h, lgeo), (ggeo_h, ggeo),
                (partners_h, partners), (peers_h, peers), (slots_h, slots),
                (offsets_h, offsets), (trow_h, trow), (tcol_h, tcol),
            ]
        )
    ]
    for c in loads:
        c.start()

    def copy(src, dst, ss, rs, peer):
        return pltpu.make_async_remote_copy(
            src_ref=src, dst_ref=dst, send_sem=ss, recv_sem=rs, device_id=peer, device_id_type=MESH
        )

    def rs_copy(a, b):
        piece = ptop.at[lax.rem(x + b, NX) * NZ + lax.rem(z + a, NZ)]
        return copy(piece, rsbuf.at[a * NX + b], sends.at[0], recvs.at[0], leaf_peer(a, b))

    def geo_copy(a, b):
        return copy(geo, geos_v.at[d], sends.at[1], recvs.at[1], leaf_peer(a, b))

    def mid_copy(step, k):
        if step == 0:
            i = x * NZ + z
            return copy(midc.at[0], mids.at[i], sends.at[2], recvs.at[2], leaf_peer(k, 0))
        if step == 1:
            i = NL + z * NX + x
            return copy(midc.at[1], mids.at[i], sends.at[9], recvs.at[9], leaf_peer(0, k))
        if step == 2:
            block = mids.at[pl.ds(x * NZ, NZ)]
            return copy(block, block, sends.at[10], recvs.at[10], leaf_peer(0, k))
        block = mids.at[pl.ds(NL + z * NX, NX)]
        return copy(block, block, sends.at[11], recvs.at[11], leaf_peer(k, 0))

    def tg_copy(k):
        return copy(tgeo, tgeos_v.at[g], sends.at[3], recvs.at[3], (lax.rem(g + k, NG), d))

    def z_copy(k):
        return copy(zbuf.at[z], zbuf.at[z], sends.at[4], recvs.at[4], leaf_peer(k, 0))

    def top_copy(a, b):
        return copy(ztile, tops.at[g * NX + x], sends.at[5], recvs.at[5], plane_peer(a, b))

    whole = [
        rsbuf.at[pl.ds(1, NL - 1)], geos_v.at[pl.ds(0, NL - 1)], mids.at[pl.ds(0, NZ - 1)],
        tgeos_v.at[pl.ds(0, NG - 1)], zbuf.at[pl.ds(0, NZ - 1)], tops.at[pl.ds(0, 31)],
        pwin.at[pl.ds(0, 2)], mwin.at[pl.ds(0, 2)], lwin.at[pl.ds(0, 8)],
        mids.at[pl.ds(0, NX - 1)], mids.at[pl.ds(0, NZ * (NX - 1))],
        mids.at[pl.ds(0, NX * (NZ - 1))],
    ]

    def got(i):
        pltpu.make_async_copy(whole[i], whole[i], recvs.at[i]).wait()

    def sent(i):
        pltpu.make_async_copy(whole[i], whole[i], sends.at[i]).wait()

    lhalo, phalo = [], []
    for side in range(2):
        part = 2 - 2 * side
        peer = (g, lax.rem(d + (NL - 1 if side == 0 else 1), NL))
        lhalo.append(
            copy(lwin.at[4:8], lwin.at[4 * part : 4 * part + 4], sends.at[8], recvs.at[8], peer)
        )
        phalo.append(copy(pwin.at[1], pwin.at[part], sends.at[6], recvs.at[6], peer))
        phalo.append(copy(mwin.at[1], mwin.at[part], sends.at[7], recvs.at[7], peer))

    lane = lax.broadcasted_iota(jnp.int32, (RHS, PTS), 1)
    for i in range(3):
        loads[i].wait()
    pieces = []
    for l in range(16):
        cols = slice(l * PTS, (l + 1) * PTS)
        m = jnp.where(lane < counts[l], rhs_s[:, cols], 0.0)
        mwin[1, :, cols] = m
        pieces.append(nt(m, basis[l]))
    for i in range(3, 8):
        loads[i].wait()
    srow = lax.broadcasted_iota(jnp.int32, (128, 128), 0) >> 4
    blk = block_of((128, 128))
    total = jnp.zeros((128, RANK), jnp.float32)
    for q in range(4):
        tile = jnp.concatenate(pieces[4 * q : 4 * q + 4], axis=1)
        lwin[4 + q] = tile
        own = jnp.full((128, 128), owner[0, 4 * q], jnp.int32)
        for b in range(1, 4):
            own = jnp.where(blk == b, owner[0, 4 * q + b], own)
        lhs = jnp.where(own == srow, jnp.concatenate([tile] * 8, axis=0), 0.0)
        total = total + nn(lhs, leaf_t[4 * q : 4 * q + 4].reshape(128, RANK))
    srow = lax.broadcasted_iota(jnp.int32, (256, 128), 0) >> 4
    blk = block_of((256, 128))
    topp = jnp.zeros((256, RANK), jnp.float32)
    for q in range(2):
        tile = jnp.concatenate(
            [total[(4 * q + b) * 16 : (4 * q + b + 1) * 16] for b in range(4)], axis=1
        )
        midc[q] = tile
        own = jnp.full((256, 128), parent[0, 4 * q], jnp.int32)
        for b in range(1, 4):
            own = jnp.where(blk == b, parent[0, 4 * q + b], own)
        lhs = jnp.where(own == srow, jnp.concatenate([tile] * 16, axis=0), 0.0)
        topp = topp + nn(lhs, mid_t[4 * q : 4 * q + 4].reshape(128, RANK))
    for q in range(4):
        tile = jnp.concatenate(
            [topp[(4 * q + b) * 16 : (4 * q + b + 1) * 16] for b in range(4)], axis=1
        )
        for i in range(8):
            ptop[q * 8 + i] = tile[2 * i : 2 * i + 2]

    for i in range(8, 17):
        loads[i].wait()
    lane1 = lax.broadcasted_iota(jnp.int32, (1, 128), 1)
    row = jnp.zeros((1, 128), jnp.float32)
    for c in range(4):
        for i in range(8):
            row = jnp.where(lane1 == c * 8 + i, mgeo[c, i], row)
        for i in range(16):
            row = jnp.where(lane1 == 32 + c * 16 + i, lgeo[c, i], row)
    geo[...] = row
    geos_v[d] = row
    row = jnp.zeros((1, 128), jnp.float32)
    for c in range(4):
        for i in range(16):
            row = jnp.where(lane1 == c * 16 + i, ggeo[c, i], row)
    tgeo[...] = row
    tgeos_v[g] = row

    def make_w(l):
        w_s[l] = dot3(leaf_t[l], basis[l], 0, 0)

    loop(16, 4, make_w)

    sub = lax.broadcasted_iota(jnp.int32, (8, PTS), 0)

    def split3(v):
        a = bf(v).astype(jnp.float32)
        r = v - a
        b = bf(r).astype(jnp.float32)
        return a, b, r - b

    def window(part, i):
        cols = pl.ds(pl.multiple_of(i * PTS, PTS), PTS)
        m = mwin[part, :, cols]
        high = bf(m)
        w = part * 16 + i
        mhl[w] = jnp.concatenate([high, bf(m - high.astype(jnp.float32))], axis=0)
        c = (pwin[part, :, cols] - 0.5) * RATE
        norm = jnp.sum(c * c, axis=0, keepdims=True)
        c8 = jnp.concatenate([c, jnp.zeros((5, PTS), jnp.float32)], axis=0)
        v = jnp.where(sub == 3, norm, jnp.where(sub == 4, 1.0, c8))
        a, b, e = split3(v)
        bwin[w] = bf(jnp.concatenate([a, a, a, b, b, e], axis=0))
        if part == 1:
            v = jnp.where(sub == 3, 1.0, jnp.where(sub == 4, norm, -2.0 * c8))
            a, b, e = split3(v)
            awin[i] = bf(jnp.concatenate([a, b, e, a, b, a], axis=0).T)

    loop(16, 4, lambda i: window(1, i))

    pl.semaphore_wait(barrier, 62)
    others(NZ, lambda a, b: rs_copy(a, b).start())
    for c in phalo:
        c.start()
    others(NZ, lambda a, b: geo_copy(a, b).start())
    each(1, NG, lambda k: tg_copy(k).start())
    for c in lhalo:
        c.start()
    each(1, NZ, lambda k: mid_copy(0, k).start())
    for k in range(1, NX):
        mid_copy(1, k).start()
    mids[x * NZ + z] = midc[0]
    mids[NL + z * NX + x] = midc[1]

    def distances(l, sb):
        for j in range(4):
            ws = [l + 16 + partners[l, 2 * j + e] for e in range(2)]
            sb[j] = raw(awin[l], jnp.concatenate([bwin[w] for w in ws], axis=1), 1, 0)

    def kernels(sb, kb):
        for j in range(4):
            k = kappa(sb[j])
            high = bf(k)
            kb[j, 0:PTS] = high
            kb[j, PTS : 2 * PTS] = bf(k - high.astype(jnp.float32))

    def products(l, kb):
        acc = jnp.zeros((2 * RHS, 2 * PTS), jnp.float32)
        for j in range(4):
            ws = [l + 16 + partners[l, 2 * j + e] for e in range(2)]
            m = jnp.concatenate([mhl[w] for w in ws], axis=1)
            acc = acc + raw(m, kb[j], 1, 1)
        base_s[l] = acc[:RHS, :PTS] + (acc[RHS:, :PTS] + acc[:RHS, PTS:])

    def near(i):
        distances(jnp.minimum(2 * i + 2, 15), sb0)
        kernels(sb1, kb1)
        products(2 * i, kb0)
        distances(jnp.minimum(2 * i + 3, 15), sb1)
        kernels(sb0, kb0)
        products(2 * i + 1, kb1)

    blk16 = block_of((RHS, 128))
    blk1 = block_of((1, 128))

    def gather(tab, srcs):
        acc = None
        for j, s in enumerate(srcs):
            t = pltpu.roll(tab[s >> 2], ((j - (s & 3)) & 3) * 32, 1)
            acc = t if j == 0 else jnp.where(blk16 == j, t, acc)
        return acc

    def target_nodes(read):
        h = read(3)
        return [(read(c) + h * tcol[c]) * RATE for c in range(3)]

    def coupling(tnodes, reads):
        def mix(c):
            v = jnp.full((1, 128), reads[0](c), jnp.float32)
            for j in range(1, 4):
                v = jnp.where(blk1 == j, reads[j](c), v)
            return v

        h = mix(3)
        squared = None
        for c in range(3):
            r = (mix(c) + h * trow[c : c + 1, :]) * RATE
            diff = tnodes[c] - r
            squared = diff * diff if squared is None else squared + diff * diff
        return kappa(squared)

    def top_read(s):
        return lambda c: tgeos[s >> 4, 0, c * 16 + (s & 15)]

    def mid_read(i):
        return lambda c: geos[i >> 3, 0, c * 8 + (i & 7)]

    def leaf_read(w):
        dev = lax.rem(d + NL - 1 + (w >> 4), NL)
        return lambda c: geos[dev, 0, 32 + c * 16 + (w & 15)]

    got(3)
    to_smem = pltpu.make_async_copy(tgeos_v, tgeos, s_in.at[1])
    to_smem.start()
    to_smem.wait()

    def top_sources(b):
        p = parent[0, b]
        t = g * 16 + p
        return t, [[(t + offsets[p, 4 * q + j]) & 127 for j in range(4)] for q in range(4)]

    def top_coupling(b):
        t, srcs = top_sources(b)
        nodes = target_nodes(top_read(t))
        s = [coupling(nodes, [top_read(i) for i in four]) for four in srcs]
        p_s[b] = nn(mid_t[b], jnp.concatenate(s, axis=1))

    loop(8, 4, top_coupling)

    got(0)
    terms = [ptop[x * 8 + z]] + [rsbuf[k] for k in range(1, NL)]
    while len(terms) > 1:
        terms = [a + b for a, b in zip(terms[::2], terms[1::2])]
    zbuf[z] = terms[0]
    each(1, NZ, lambda k: z_copy(k).start())
    got(2)
    got(9)
    for k in range(1, NX):
        mid_copy(2, k).start()
    each(1, NZ, lambda k: mid_copy(3, k).start())
    got(6)
    got(7)
    loop(16, 4, lambda i: window(0, i))
    loop(16, 4, lambda i: window(2, i))
    distances(0, sb0)
    kernels(sb0, kb0)
    distances(1, sb1)
    each(0, N2, near)
    got(4)
    for i in range(8):
        ztile[2 * i : 2 * i + 2] = zbuf[i]
    others(NG, lambda a, b: top_copy(a, b).start())
    tops[g * NX + x] = ztile[...]
    each(N2, 8, near)

    got(1)
    got(8)
    to_smem = pltpu.make_async_copy(geos_v, geos, s_in.at[0])
    to_smem.start()
    to_smem.wait()

    def leaf_far(l):
        nodes = target_nodes(leaf_read(l + 16))
        cs, ss = [], []
        for q in range(2):
            srcs = [l + 16 + partners[l, 8 + 4 * q + j] for j in range(4)]
            cs.append(gather(lwin, srcs))
            ss.append(coupling(nodes, [leaf_read(s) for s in srcs]))
        local = nt(jnp.concatenate(cs, axis=1), jnp.concatenate(ss, axis=1))
        far_l[l] = nn(local, basis[l])

    loop(16, 4, leaf_far)

    got(10)
    got(11)

    def mid_coupling(b):
        nodes = target_nodes(mid_read(d * 8 + b))
        cs, ss = [], []
        for q in range(2):
            named = [(peers[b, 4 * q + j], slots[b, 4 * q + j]) for j in range(4)]
            srcs = [p * 8 + i for p, i in named]
            places = [
                jnp.where(i < 4, (p & 3) * NZ + (p >> 2), NL + p) * 4 + (i & 3) for p, i in named
            ]
            cs.append(gather(mids, places))
            ss.append(coupling(nodes, [mid_read(s) for s in srcs]))
        far_m[b] = nt(jnp.concatenate(cs, axis=1), jnp.concatenate(ss, axis=1))

    loop(8, 4, mid_coupling)

    got(5)

    def down_mid(b):
        _, srcs = top_sources(b)
        c = jnp.concatenate([gather(tops, four) for four in srcs], axis=1)
        mid_s[b] = far_m[b] + nt(c, p_s[b])

    loop(8, 4, down_mid)

    for l in range(16):
        cols = slice(l * PTS, (l + 1) * PTS)
        value = base_s[l] + far_l[l] + nn(mid_s[owner[0, l]], w_s[l])
        out[:, cols] = value

    for i in range(12):
        sent(i)


N2 = 4
VM = pl.BlockSpec(memory_space=pltpu.VMEM)
SM = pl.BlockSpec(memory_space=pltpu.SMEM)
ANY = pl.BlockSpec(memory_space=pl.ANY)


def on_device(
    points, rhs, counts, basis, leaf_geom, leaf_partners, leaf_middle_owner, leaf_basis_transfer,
    mid_geom, mid_parent, mid_transfer, mid_peers, mid_slots, top_geom, top_offsets,
):
    table = node_table()
    trow = np.zeros((8, 128), np.float32)
    trow[:3] = np.tile(table, (1, 4))
    tcol = np.broadcast_to(table[:, :, None], (3, 32, 128)).astype(np.float32)
    dma = pltpu.SemaphoreType.DMA

    def vm(*shape, dtype=jnp.float32):
        return pltpu.VMEM(shape, dtype)

    def sm(*shape, dtype=jnp.int32):
        return pltpu.SMEM(shape, dtype)

    product = pl.pallas_call(
        whole_kernel,
        out_shape=pltpu.VMEM((16, 2048), jnp.float32),
        in_specs=[ANY] * 17,
        out_specs=VM,
        scratch_shapes=[
            sm(16), sm(1, 16), sm(1, 8), sm(16, 16), sm(8, 8), sm(8, 8), sm(16, 16),
            sm(4, 8, dtype=jnp.float32), sm(4, 16, dtype=jnp.float32),
            sm(4, 16, dtype=jnp.float32), vm(8, 128), vm(3, 32, 128),
            vm(16, 2048), vm(16, 32, 128), vm(16, 32, 32), vm(8, 32, 32),
            vm(3, 16, 2048), vm(3, 3, 2048), vm(12, 16, 128), vm(2, 16, 128), vm(32, 2, 128),
            vm(1, 128), vm(1, 128),
            vm(64, 16, 128), pltpu.SMEM((32, 1, 128), jnp.float32),
            pltpu.SMEM((8, 1, 128), jnp.float32), vm(32, 16, 128),
            vm(32, 2, 128), vm(8, 2, 128), vm(16, 128),
            vm(48, 32, 128, dtype=jnp.bfloat16), vm(16, 128, 48, dtype=jnp.bfloat16),
            vm(48, 48, 128, dtype=jnp.bfloat16), vm(4, 128, 256), vm(4, 128, 256),
            vm(4, 256, 256, dtype=jnp.bfloat16),
            vm(4, 256, 256, dtype=jnp.bfloat16),
            vm(16, 16, 128), vm(16, 16, 128), vm(8, 16, 32), vm(8, 32, 512), vm(16, 32, 128), vm(8, 16, 32),
            vm(32, 1, 128), vm(8, 1, 128),
            dma((17,)), dma((12,)), dma((12,)),
        ],
        compiler_params=pltpu.CompilerParams(collective_id=0, has_side_effects=True),
        name="whole",
    )(
        counts, leaf_middle_owner, mid_parent, leaf_partners, mid_peers, mid_slots, top_offsets,
        mid_geom.T, leaf_geom.T, top_geom.T,
        points, rhs, jnp.swapaxes(basis, 1, 2), leaf_basis_transfer, mid_transfer,
        jnp.asarray(trow), jnp.asarray(tcol),
    )
    return pl.pallas_call(
        mask_kernel,
        out_shape=jax.ShapeDtypeStruct((16, 2048), jnp.float32),
        in_specs=[SM, VM],
        out_specs=VM,
        name="mask",
    )(counts, pltpu.with_memory_space_constraint(product, pltpu.VMEM))


def solution(mesh):
    both = ("group", "leaf")
    placed = (
        P(None, both), P(None, both), P(both), P(both, None, None), P(both, None), P(both, None),
        P(both, None), P(both, None, None), P(both, None), P("group", "leaf"), P(both, None, None),
        P(both, None), P(both, None), P("group", None), P("group", None),
    )
    return jax.shard_map(
        on_device, mesh=mesh, in_specs=placed, out_specs=P(None, both), check_vma=False
    )
```

```python
import functools

import jax
import jax.numpy as jnp
import numpy as np
from jax import lax
from jax.experimental import pallas as pl
from jax.experimental.pallas import tpu as pltpu
from jax.sharding import PartitionSpec as P

MESH = pl.DeviceIdType.MESH
PTS = 128
RANK = 32
RHS = 16
RATE = 1.7320508075688772 / 0.5
NX = 4
NZ = 8
NL = 32
NG = 8


def node_table():
    k = np.arange(RANK)
    rows = [
        np.cos(np.pi * (((k * (2 * d + 3)) % RANK) + 0.5) / RANK) for d in range(3)
    ]
    return np.stack(rows).astype(np.float32)


def bf(a):
    return a.astype(jnp.bfloat16)


def raw(a, b, ca, cb):
    return lax.dot_general(
        a, b, (((ca,), (cb,)), ((), ())), preferred_element_type=jnp.float32
    )


def dot3(a, b, ca, cb):
    ah, bh = bf(a), bf(b)
    al, bl = bf(a - ah.astype(jnp.float32)), bf(b - bh.astype(jnp.float32))
    return raw(ah, bh, ca, cb) + (raw(al, bh, ca, cb) + raw(ah, bl, ca, cb))


def nt(a, b):
    return dot3(a, b, 1, 1)


def nn(a, b):
    return dot3(a, b, 1, 0)


def kappa(squared):
    squared = jnp.maximum(squared, 1e-30)
    t = squared * lax.rsqrt(squared)
    return (1.0 + t) * jnp.exp2(t * -1.4426950408889634)


def block_of(shape):
    return lax.broadcasted_iota(jnp.int32, shape, 1) >> 5


def loop(count, width, f):
    def step(i, c):
        for e in range(width):
            f(i * width + e)
        return c

    lax.fori_loop(0, count // width, step, 0)


def store_kernel(product, out, sems):
    parts = [
        pltpu.make_async_copy(product.at[8 * i : 8 * i + 8], out.at[8 * i : 8 * i + 8], sems.at[i])
        for i in range(2)
    ]
    for c in parts:
        c.start()
    for c in parts:
        c.wait()


def whole_kernel(
    counts_h, owner_h, parent_h, partners_h, peers_h, slots_h, offsets_h, mgeo_h, lgeo_h, ggeo_h,
    points, rhs, basis_h, leaf_h, mid_h, trow_h, tcol_h,
    out,
    counts, owner, parent, partners, peers, slots, offsets, mgeo, lgeo, ggeo, trow, tcol,
    rhs_s, basis, leaf_t, mid_t, mwin, pwin, lwin, midc, ptop, geo, tgeo,
    mids, geos, tgeos, lgeos, tops, rsbuf, zbuf, ztile,
    mhl, awin, bwin, sb0, sb1, kb0, kb1, base_s, far_l, far_m, p_s, w_s, mid_s, geos_v, tgeos_v, lgeos_v,
    s_in, sends, recvs,
):
    g = lax.axis_index("group")
    d = lax.axis_index("leaf")
    z = d // NX
    x = d % NX

    y = g // 2
    core = g % 2
    xs = [x] + [lax.rem(x + b, NX) for b in range(1, NX)]
    zs = [z] + [lax.rem(z + a, NZ) for a in range(1, NZ)]
    ys = [y] + [lax.rem(y + a, 4) for a in range(1, 4)]
    cs = [core, 1 - core]

    def leaf_peer(a, b):
        return (g, zs[a] * NX + xs[b])

    def plane_peer(a, b):
        return (ys[a // 2] * 2 + cs[a % 2], z * NX + xs[b])

    def each(lo, hi, f):
        def step(k, c):
            f(k)
            return c

        lax.fori_loop(lo, hi, step, 0)

    def others(count, f):
        def hops(a, b):
            along = min(a, NZ - a) if count == NZ else min(a // 2, 4 - a // 2)
            return along + min(b, NX - b)

        pairs = [(a, b) for a in range(8) for b in range(NX) if (a, b) != (0, 0)]
        for a, b in sorted(pairs, key=lambda p: -hops(*p)):
            f(a, b)

    barrier = pltpu.get_barrier_semaphore()

    def hello(peer):
        pl.semaphore_signal(barrier, inc=1, device_id=peer, device_id_type=MESH)

    others(NZ, lambda a, b: hello(leaf_peer(a, b)))
    others(-1, lambda a, b: hello(plane_peer(a, b)))

    loads = [
        pltpu.make_async_copy(a, b, s_in.at[i])
        for i, (a, b) in enumerate(
            [
                (counts_h, counts), (rhs, rhs_s), (basis_h, basis), (owner_h, owner),
                (parent_h, parent), (leaf_h, leaf_t), (mid_h, mid_t), (points, pwin.at[1]),
                (mgeo_h, mgeo), (lgeo_h, lgeo), (ggeo_h, ggeo),
                (partners_h, partners), (peers_h, peers), (slots_h, slots),
                (offsets_h, offsets), (trow_h, trow), (tcol_h, tcol),
            ]
        )
    ]
    for c in loads:
        c.start()

    def copy(src, dst, ss, rs, peer):
        return pltpu.make_async_remote_copy(
            src_ref=src, dst_ref=dst, send_sem=ss, recv_sem=rs, device_id=peer, device_id_type=MESH
        )

    def rs_copy(a, b):
        piece = ptop.at[xs[b] * NZ + zs[a]]
        return copy(piece, rsbuf.at[a * NX + b], sends.at[0], recvs.at[0], leaf_peer(a, b))

    def geo_copy(a, b):
        return copy(geo, geos_v.at[d], sends.at[1], recvs.at[1], leaf_peer(a, b))

    def mid_copy(step, k):
        if step == 0:
            i = x * NZ + z
            return copy(midc.at[0], mids.at[i], sends.at[2], recvs.at[2], leaf_peer(k, 0))
        if step == 1:
            i = NL + z * NX + x
            return copy(midc.at[1], mids.at[i], sends.at[9], recvs.at[9], leaf_peer(0, k))
        if step == 2:
            block = mids.at[pl.ds(x * NZ, NZ)]
            return copy(block, block, sends.at[10], recvs.at[10], leaf_peer(0, k))
        block = mids.at[pl.ds(NL + z * NX, NX)]
        return copy(block, block, sends.at[11], recvs.at[11], leaf_peer(k, 0))

    def tg_copy(k):
        return copy(tgeo, tgeos_v.at[g], sends.at[3], recvs.at[3], (lax.rem(g + k, NG), d))

    def z_copy(k):
        return copy(zbuf.at[z], zbuf.at[z], sends.at[4], recvs.at[4], leaf_peer(k, 0))

    def ring(f):
        for k in (4, 3, 5, 2, 6, 1, 7):
            f(k)

    def top_copy(a, b):
        return copy(ztile, tops.at[g * NX + x], sends.at[5], recvs.at[5], plane_peer(a, b))

    whole = [
        rsbuf.at[pl.ds(1, NL - 1)], geos_v.at[pl.ds(0, NL - 1)], mids.at[pl.ds(0, NZ - 1)],
        tgeos_v.at[pl.ds(0, NG - 1)], zbuf.at[pl.ds(0, NZ - 1)], tops.at[pl.ds(0, 31)],
        pwin.at[pl.ds(0, 2)], mwin.at[pl.ds(0, 2)], lwin.at[pl.ds(0, 8)],
        mids.at[pl.ds(0, NX - 1)], mids.at[pl.ds(0, NZ * (NX - 1))],
        mids.at[pl.ds(0, NX * (NZ - 1))], lgeos_v.at[pl.ds(0, 2)],
    ]

    def got(i):
        pltpu.make_async_copy(whole[i], whole[i], recvs.at[i]).wait()

    def sent(i):
        pltpu.make_async_copy(whole[i], whole[i], sends.at[i]).wait()

    lhalo, phalo = [], []
    for side in range(2):
        part = 2 - 2 * side
        peer = (g, lax.rem(d + (NL - 1 if side == 0 else 1), NL))
        lhalo.append(
            copy(lwin.at[4:8], lwin.at[4 * part : 4 * part + 4], sends.at[8], recvs.at[8], peer)
        )
        lhalo.append(copy(geo, lgeos_v.at[part], sends.at[12], recvs.at[12], peer))
        phalo.append(copy(pwin.at[1], pwin.at[part], sends.at[6], recvs.at[6], peer))
        phalo.append(copy(mwin.at[1], mwin.at[part], sends.at[7], recvs.at[7], peer))

    lane = lax.broadcasted_iota(jnp.int32, (RHS, PTS), 1)
    for i in range(3):
        loads[i].wait()
    pieces = []
    for l in range(16):
        cols = slice(l * PTS, (l + 1) * PTS)
        m = jnp.where(lane < counts[l], rhs_s[:, cols], 0.0)
        mwin[1, :, cols] = m
        pieces.append(nt(m, basis[l]))
    for i in range(3, 8):
        loads[i].wait()
    srow = lax.broadcasted_iota(jnp.int32, (128, 128), 0) >> 4
    blk = block_of((128, 128))
    total = jnp.zeros((128, RANK), jnp.float32)
    for q in range(4):
        tile = jnp.concatenate(pieces[4 * q : 4 * q + 4], axis=1)
        lwin[4 + q] = tile
        own = jnp.full((128, 128), owner[0, 4 * q], jnp.int32)
        for b in range(1, 4):
            own = jnp.where(blk == b, owner[0, 4 * q + b], own)
        lhs = jnp.where(own == srow, jnp.concatenate([tile] * 8, axis=0), 0.0)
        total = total + nn(lhs, leaf_t[4 * q : 4 * q + 4].reshape(128, RANK))
    srow = lax.broadcasted_iota(jnp.int32, (256, 128), 0) >> 4
    blk = block_of((256, 128))
    topp = jnp.zeros((256, RANK), jnp.float32)
    for q in range(2):
        tile = jnp.concatenate(
            [total[(4 * q + b) * 16 : (4 * q + b + 1) * 16] for b in range(4)], axis=1
        )
        midc[q] = tile
        own = jnp.full((256, 128), parent[0, 4 * q], jnp.int32)
        for b in range(1, 4):
            own = jnp.where(blk == b, parent[0, 4 * q + b], own)
        lhs = jnp.where(own == srow, jnp.concatenate([tile] * 16, axis=0), 0.0)
        topp = topp + nn(lhs, mid_t[4 * q : 4 * q + 4].reshape(128, RANK))
    for q in range(4):
        tile = jnp.concatenate(
            [topp[(4 * q + b) * 16 : (4 * q + b + 1) * 16] for b in range(4)], axis=1
        )
        for i in range(8):
            ptop[q * 8 + i] = tile[2 * i : 2 * i + 2]

    for i in range(8, 17):
        loads[i].wait()
    lane1 = lax.broadcasted_iota(jnp.int32, (1, 128), 1)
    row = jnp.zeros((1, 128), jnp.float32)
    for c in range(4):
        for i in range(8):
            row = jnp.where(lane1 == c * 8 + i, mgeo[c, i], row)
        for i in range(16):
            row = jnp.where(lane1 == 32 + c * 16 + i, lgeo[c, i], row)
    geo[...] = row
    geos_v[d] = row
    lgeos_v[1] = row
    row = jnp.zeros((1, 128), jnp.float32)
    for c in range(4):
        for i in range(16):
            row = jnp.where(lane1 == c * 16 + i, ggeo[c, i], row)
    tgeo[...] = row
    tgeos_v[g] = row

    def make_w(l):
        w_s[l] = dot3(leaf_t[l], basis[l], 0, 0)

    loop(16, 4, make_w)

    sub = lax.broadcasted_iota(jnp.int32, (8, PTS), 0)

    def split3(v):
        a = bf(v).astype(jnp.float32)
        r = v - a
        b = bf(r).astype(jnp.float32)
        return a, b, r - b

    def window(part, i):
        cols = pl.ds(pl.multiple_of(i * PTS, PTS), PTS)
        m = mwin[part, :, cols]
        high = bf(m)
        w = part * 16 + i
        mhl[w] = jnp.concatenate([high, bf(m - high.astype(jnp.float32))], axis=0)
        c = (pwin[part, :, cols] - 0.5) * RATE
        norm = jnp.sum(c * c, axis=0, keepdims=True)
        c8 = jnp.concatenate([c, jnp.zeros((5, PTS), jnp.float32)], axis=0)
        v = jnp.where(sub == 3, norm, jnp.where(sub == 4, 1.0, c8))
        a, b, e = split3(v)
        bwin[w] = bf(jnp.concatenate([a, a, a, b, b, e], axis=0))
        if part == 1:
            v = jnp.where(sub == 3, 1.0, jnp.where(sub == 4, norm, -2.0 * c8))
            a, b, e = split3(v)
            awin[i] = bf(jnp.concatenate([a, b, e, a, b, a], axis=0).T)

    loop(16, 4, lambda i: window(1, i))

    pl.semaphore_wait(barrier, 62)
    others(NZ, lambda a, b: rs_copy(a, b).start())
    each(1, NG, lambda k: tg_copy(k).start())
    for c in lhalo:
        c.start()
    for c in phalo:
        c.start()
    others(NZ, lambda a, b: geo_copy(a, b).start())
    ring(lambda k: mid_copy(0, k).start())
    for k in range(1, NX):
        mid_copy(1, k).start()
    mids[x * NZ + z] = midc[0]
    mids[NL + z * NX + x] = midc[1]

    def distances(l, sb):
        for j in range(4):
            ws = [l + 16 + partners[l, 2 * j + e] for e in range(2)]
            sb[j] = raw(awin[l], jnp.concatenate([bwin[w] for w in ws], axis=1), 1, 0)

    def kernels(sb, kb):
        for j in range(4):
            k = kappa(sb[j])
            high = bf(k)
            kb[j, 0:PTS] = high
            kb[j, PTS : 2 * PTS] = bf(k - high.astype(jnp.float32))

    def products(l, kb):
        acc = jnp.zeros((2 * RHS, 2 * PTS), jnp.float32)
        for j in range(4):
            ws = [l + 16 + partners[l, 2 * j + e] for e in range(2)]
            m = jnp.concatenate([mhl[w] for w in ws], axis=1)
            acc = acc + raw(m, kb[j], 1, 1)
        base_s[l] = acc[:RHS, :PTS] + (acc[RHS:, :PTS] + acc[:RHS, PTS:])

    def near(i):
        distances(jnp.minimum(2 * i + 2, 15), sb0)
        kernels(sb1, kb1)
        products(2 * i, kb0)
        distances(jnp.minimum(2 * i + 3, 15), sb1)
        kernels(sb0, kb0)
        products(2 * i + 1, kb1)

    blk16 = block_of((RHS, 128))
    blk1 = block_of((1, 128))

    def gather(tab, srcs):
        acc = None
        for j, s in enumerate(srcs):
            t = pltpu.roll(tab[s >> 2], ((j - (s & 3)) & 3) * 32, 1)
            acc = t if j == 0 else jnp.where(blk16 == j, t, acc)
        return acc

    def target_nodes(read):
        h = read(3)
        return [(read(c) + h * tcol[c]) * RATE for c in range(3)]

    def coupling(tnodes, reads):
        def mix(c):
            v = jnp.full((1, 128), reads[0](c), jnp.float32)
            for j in range(1, 4):
                v = jnp.where(blk1 == j, reads[j](c), v)
            return v

        h = mix(3)
        squared = None
        for c in range(3):
            r = (mix(c) + h * trow[c : c + 1, :]) * RATE
            diff = tnodes[c] - r
            squared = diff * diff if squared is None else squared + diff * diff
        return kappa(squared)

    def top_read(s):
        return lambda c: tgeos[s >> 4, 0, c * 16 + (s & 15)]

    def mid_read(i):
        return lambda c: geos[i >> 3, 0, c * 8 + (i & 7)]

    def leaf_read(w):
        return lambda c: lgeos[w >> 4, 0, 32 + c * 16 + (w & 15)]

    got(3)
    to_smem = pltpu.make_async_copy(tgeos_v, tgeos, s_in.at[1])
    to_smem.start()
    to_smem.wait()

    def top_sources(b):
        p = parent[0, b]
        t = g * 16 + p
        return t, [[(t + offsets[p, 4 * q + j]) & 127 for j in range(4)] for q in range(4)]

    def top_coupling(b):
        t, srcs = top_sources(b)
        nodes = target_nodes(top_read(t))
        s = [coupling(nodes, [top_read(i) for i in four]) for four in srcs]
        p_s[b] = nn(mid_t[b], jnp.concatenate(s, axis=1))

    loop(8, 4, top_coupling)

    got(8)
    got(12)
    to_smem = pltpu.make_async_copy(lgeos_v, lgeos, s_in.at[0])
    to_smem.start()
    to_smem.wait()
    def leaf_far(l):
        nodes = target_nodes(leaf_read(l + 16))
        cs, ss = [], []
        for q in range(2):
            srcs = [l + 16 + partners[l, 8 + 4 * q + j] for j in range(4)]
            cs.append(gather(lwin, srcs))
            ss.append(coupling(nodes, [leaf_read(s) for s in srcs]))
        local = nt(jnp.concatenate(cs, axis=1), jnp.concatenate(ss, axis=1))
        far_l[l] = nn(local, basis[l])

    def leaf_four(q):
        for e in range(4):
            leaf_far(4 * q + e)

    each(0, 1, leaf_four)
    got(0)
    terms = [ptop[x * 8 + z]] + [rsbuf[k] for k in range(1, NL)]
    while len(terms) > 1:
        terms = [a + b for a, b in zip(terms[::2], terms[1::2])]
    zbuf[z] = terms[0]
    ring(lambda k: z_copy(k).start())
    got(2)
    got(9)
    for k in range(1, NX):
        mid_copy(2, k).start()
    ring(lambda k: mid_copy(3, k).start())
    each(1, 4, leaf_four)
    got(6)
    got(7)
    loop(16, 4, lambda i: window(0, i))
    loop(16, 4, lambda i: window(2, i))
    distances(0, sb0)
    kernels(sb0, kb0)
    distances(1, sb1)
    each(0, N2, near)
    got(4)
    for i in range(8):
        ztile[2 * i : 2 * i + 2] = zbuf[i]
    others(-1, lambda a, b: top_copy(a, b).start())
    tops[g * NX + x] = ztile[...]
    each(N2, 8, near)

    got(1)
    to_smem = pltpu.make_async_copy(geos_v, geos, s_in.at[0])
    to_smem.start()
    to_smem.wait()

    got(10)
    got(11)

    def mid_coupling(b):
        nodes = target_nodes(mid_read(d * 8 + b))
        cs, ss = [], []
        for q in range(2):
            named = [(peers[b, 4 * q + j], slots[b, 4 * q + j]) for j in range(4)]
            srcs = [p * 8 + i for p, i in named]
            places = [
                jnp.where(i < 4, (p & 3) * NZ + (p >> 2), NL + p) * 4 + (i & 3) for p, i in named
            ]
            cs.append(gather(mids, places))
            ss.append(coupling(nodes, [mid_read(s) for s in srcs]))
        far_m[b] = nt(jnp.concatenate(cs, axis=1), jnp.concatenate(ss, axis=1))

    loop(8, 4, mid_coupling)

    got(5)

    def down_mid(b):
        _, srcs = top_sources(b)
        c = jnp.concatenate([gather(tops, four) for four in srcs], axis=1)
        mid_s[b] = far_m[b] + nt(c, p_s[b])

    loop(8, 4, down_mid)

    for l in range(16):
        cols = slice(l * PTS, (l + 1) * PTS)
        value = base_s[l] + far_l[l] + nn(mid_s[owner[0, l]], w_s[l])
        out[:, cols] = jnp.where(lane < counts[l], value, 0.0)

    for i in range(13):
        sent(i)


N2 = 1
VM = pl.BlockSpec(memory_space=pltpu.VMEM)
ANY = pl.BlockSpec(memory_space=pl.ANY)


def on_device(
    points, rhs, counts, basis, leaf_geom, leaf_partners, leaf_middle_owner, leaf_basis_transfer,
    mid_geom, mid_parent, mid_transfer, mid_peers, mid_slots, top_geom, top_offsets,
):
    table = node_table()
    trow = np.zeros((8, 128), np.float32)
    trow[:3] = np.tile(table, (1, 4))
    tcol = np.broadcast_to(table[:, :, None], (3, 32, 128)).astype(np.float32)
    dma = pltpu.SemaphoreType.DMA

    def vm(*shape, dtype=jnp.float32):
        return pltpu.VMEM(shape, dtype)

    def sm(*shape, dtype=jnp.int32):
        return pltpu.SMEM(shape, dtype)

    product = pl.pallas_call(
        whole_kernel,
        out_shape=pltpu.VMEM((16, 2048), jnp.float32),
        in_specs=[ANY] * 17,
        out_specs=VM,
        scratch_shapes=[
            sm(16), sm(1, 16), sm(1, 8), sm(16, 16), sm(8, 8), sm(8, 8), sm(16, 16),
            sm(4, 8, dtype=jnp.float32), sm(4, 16, dtype=jnp.float32),
            sm(4, 16, dtype=jnp.float32), vm(8, 128), vm(3, 32, 128),
            vm(16, 2048), vm(16, 32, 128), vm(16, 32, 32), vm(8, 32, 32),
            vm(3, 16, 2048), vm(3, 3, 2048), vm(12, 16, 128), vm(2, 16, 128), vm(32, 2, 128),
            vm(1, 128), vm(1, 128),
            vm(64, 16, 128), pltpu.SMEM((32, 1, 128), jnp.float32),
            pltpu.SMEM((8, 1, 128), jnp.float32),
            pltpu.SMEM((3, 1, 128), jnp.float32), vm(32, 16, 128),
            vm(32, 2, 128), vm(8, 2, 128), vm(16, 128),
            vm(48, 32, 128, dtype=jnp.bfloat16), vm(16, 128, 48, dtype=jnp.bfloat16),
            vm(48, 48, 128, dtype=jnp.bfloat16), vm(4, 128, 256), vm(4, 128, 256),
            vm(4, 256, 256, dtype=jnp.bfloat16),
            vm(4, 256, 256, dtype=jnp.bfloat16),
            vm(16, 16, 128), vm(16, 16, 128), vm(8, 16, 32), vm(8, 32, 512), vm(16, 32, 128), vm(8, 16, 32),
            vm(32, 1, 128), vm(8, 1, 128), vm(3, 1, 128),
            dma((17,)), dma((13,)), dma((13,)),
        ],
        compiler_params=pltpu.CompilerParams(collective_id=0, has_side_effects=True),
        name="whole",
    )(
        counts, leaf_middle_owner, mid_parent, leaf_partners, mid_peers, mid_slots, top_offsets,
        mid_geom.T, leaf_geom.T, top_geom.T,
        points, rhs, jnp.swapaxes(basis, 1, 2), leaf_basis_transfer, mid_transfer,
        jnp.asarray(trow), jnp.asarray(tcol),
    )
    return pl.pallas_call(
        store_kernel,
        out_shape=jax.ShapeDtypeStruct((16, 2048), jnp.float32),
        in_specs=[VM],
        out_specs=ANY,
        scratch_shapes=[dma((2,))],
        name="store",
    )(pltpu.with_memory_space_constraint(product, pltpu.VMEM))


def solution(mesh):
    both = ("group", "leaf")
    placed = (
        P(None, both), P(None, both), P(both), P(both, None, None), P(both, None), P(both, None),
        P(both, None), P(both, None, None), P(both, None), P("group", "leaf"), P(both, None, None),
        P(both, None), P(both, None), P("group", None), P("group", None),
    )
    return jax.shard_map(
        on_device, mesh=mesh, in_specs=placed, out_specs=P(None, both), check_vma=False
    )
```

```python
import functools

import jax
import jax.numpy as jnp
import numpy as np
from jax import lax
from jax.experimental import pallas as pl
from jax.experimental.pallas import tpu as pltpu
from jax.sharding import PartitionSpec as P

MESH = pl.DeviceIdType.MESH
PTS = 128
RANK = 32
RHS = 16
RATE = 1.7320508075688772 / 0.5
NX = 4
NZ = 8
NL = 32
NG = 8


def node_table():
    k = np.arange(RANK)
    rows = [
        np.cos(np.pi * (((k * (2 * d + 3)) % RANK) + 0.5) / RANK) for d in range(3)
    ]
    return np.stack(rows).astype(np.float32)


def bf(a):
    return a.astype(jnp.bfloat16)


def raw(a, b, ca, cb):
    return lax.dot_general(
        a, b, (((ca,), (cb,)), ((), ())), preferred_element_type=jnp.float32
    )


def dot3(a, b, ca, cb):
    ah, bh = bf(a), bf(b)
    al, bl = bf(a - ah.astype(jnp.float32)), bf(b - bh.astype(jnp.float32))
    return raw(ah, bh, ca, cb) + (raw(al, bh, ca, cb) + raw(ah, bl, ca, cb))


def split(a):
    high = bf(a)
    return high, bf(a - high.astype(jnp.float32))


def dot3_split(a, bh, bl, ca, cb):
    ah, al = split(a)
    return raw(ah, bh, ca, cb) + (raw(al, bh, ca, cb) + raw(ah, bl, ca, cb))


def nt(a, b):
    return dot3(a, b, 1, 1)


def nn(a, b):
    return dot3(a, b, 1, 0)


def kappa(squared):
    squared = jnp.maximum(squared, 1e-30)
    t = squared * lax.rsqrt(squared)
    return (1.0 + t) * jnp.exp2(t * -1.4426950408889634)


def block_of(shape):
    return lax.broadcasted_iota(jnp.int32, shape, 1) >> 5


def loop(count, width, f):
    def step(i, c):
        for e in range(width):
            f(i * width + e)
        return c

    lax.fori_loop(0, count // width, step, 0)


def store_kernel(product, out, sems):
    parts = [
        pltpu.make_async_copy(product.at[8 * i : 8 * i + 8], out.at[8 * i : 8 * i + 8], sems.at[i])
        for i in range(2)
    ]
    for c in parts:
        c.start()
    for c in parts:
        c.wait()


def whole_kernel(
    counts_h, owner_h, parent_h, partners_h, peers_h, slots_h, offsets_h, mgeo_h, lgeo_h, ggeo_h,
    points, rhs, basis_h, leaf_h, mid_h, trow_h, tcol_h,
    out,
    counts, owner, parent, partners, peers, slots, offsets, mgeo, lgeo, ggeo, trow, tcol,
    rhs_s, basis, leaf_t, mid_t, mwin, pwin, lwin, midc, ptop, geo, tgeo,
    mids, geos, tgeos, lgeos, tops, rsbuf, zbuf, ztile,
    mhl, awin, bwin, sb0, sb1, kb0, kb1, base_s, far_l, far_m, p_h, p_l, w_h, w_l, mid_s, geos_v, tgeos_v, lgeos_v,
    s_in, sends, recvs,
):
    g = lax.axis_index("group")
    d = lax.axis_index("leaf")
    z = d // NX
    x = d % NX

    y = g // 2
    core = g % 2
    xs = [x] + [lax.rem(x + b, NX) for b in range(1, NX)]
    zs = [z] + [lax.rem(z + a, NZ) for a in range(1, NZ)]
    ys = [y] + [lax.rem(y + a, 4) for a in range(1, 4)]
    cs = [core, 1 - core]

    def leaf_peer(a, b):
        return (g, zs[a] * NX + xs[b])

    def plane_peer(a, b):
        return (ys[a // 2] * 2 + cs[a % 2], z * NX + xs[b])

    def each(lo, hi, f):
        def step(k, c):
            f(k)
            return c

        lax.fori_loop(lo, hi, step, 0)

    def others(count, f):
        def hops(a, b):
            along = min(a, NZ - a) if count == NZ else min(a // 2, 4 - a // 2)
            return along + min(b, NX - b)

        pairs = [(a, b) for a in range(8) for b in range(NX) if (a, b) != (0, 0)]
        for a, b in sorted(pairs, key=lambda p: -hops(*p)):
            f(a, b)

    barrier = pltpu.get_barrier_semaphore()

    def hello(peer):
        pl.semaphore_signal(barrier, inc=1, device_id=peer, device_id_type=MESH)

    others(NZ, lambda a, b: hello(leaf_peer(a, b)))
    others(-1, lambda a, b: hello(plane_peer(a, b)))

    loads = [
        pltpu.make_async_copy(a, b, s_in.at[i])
        for i, (a, b) in enumerate(
            [
                (counts_h, counts), (rhs, rhs_s), (basis_h, basis), (owner_h, owner),
                (parent_h, parent), (leaf_h, leaf_t), (mid_h, mid_t), (points, pwin.at[1]),
                (mgeo_h, mgeo), (lgeo_h, lgeo), (ggeo_h, ggeo),
                (partners_h, partners), (peers_h, peers), (slots_h, slots),
                (offsets_h, offsets), (trow_h, trow), (tcol_h, tcol),
            ]
        )
    ]
    for c in loads:
        c.start()

    def copy(src, dst, ss, rs, peer):
        return pltpu.make_async_remote_copy(
            src_ref=src, dst_ref=dst, send_sem=ss, recv_sem=rs, device_id=peer, device_id_type=MESH
        )

    def rs_copy(a, b):
        piece = ptop.at[xs[b] * NZ + zs[a]]
        return copy(piece, rsbuf.at[a * NX + b], sends.at[0], recvs.at[0], leaf_peer(a, b))

    def geo_copy(a, b):
        return copy(geo, geos_v.at[d], sends.at[1], recvs.at[1], leaf_peer(a, b))

    def mid_copy(step, k):
        if step == 0:
            i = x * NZ + z
            return copy(midc.at[0], mids.at[i], sends.at[2], recvs.at[2], leaf_peer(k, 0))
        if step == 1:
            i = NL + z * NX + x
            return copy(midc.at[1], mids.at[i], sends.at[9], recvs.at[9], leaf_peer(0, k))
        if step == 2:
            block = mids.at[pl.ds(x * NZ, NZ)]
            return copy(block, block, sends.at[10], recvs.at[10], leaf_peer(0, k))
        block = mids.at[pl.ds(NL + z * NX, NX)]
        return copy(block, block, sends.at[11], recvs.at[11], leaf_peer(k, 0))

    def tg_copy(k):
        return copy(tgeo, tgeos_v.at[g], sends.at[3], recvs.at[3], (lax.rem(g + k, NG), d))

    def z_copy(k):
        return copy(zbuf.at[z], zbuf.at[z], sends.at[4], recvs.at[4], leaf_peer(k, 0))

    def ring(f):
        for k in (4, 3, 5, 2, 6, 1, 7):
            f(k)

    def top_copy(a, b):
        return copy(ztile, tops.at[g * NX + x], sends.at[5], recvs.at[5], plane_peer(a, b))

    whole = [
        rsbuf.at[pl.ds(1, NL - 1)], geos_v.at[pl.ds(0, NL - 1)], mids.at[pl.ds(0, NZ - 1)],
        tgeos_v.at[pl.ds(0, NG - 1)], zbuf.at[pl.ds(0, NZ - 1)], tops.at[pl.ds(0, 31)],
        pwin.at[pl.ds(0, 2)], mwin.at[pl.ds(0, 2)], lwin.at[pl.ds(0, 8)],
        mids.at[pl.ds(0, NX - 1)], mids.at[pl.ds(0, NZ * (NX - 1))],
        mids.at[pl.ds(0, NX * (NZ - 1))], lgeos_v.at[pl.ds(0, 2)],
    ]

    def got(i):
        pltpu.make_async_copy(whole[i], whole[i], recvs.at[i]).wait()

    def sent(i):
        pltpu.make_async_copy(whole[i], whole[i], sends.at[i]).wait()

    lhalo, phalo = [], []
    for side in range(2):
        part = 2 - 2 * side
        peer = (g, lax.rem(d + (NL - 1 if side == 0 else 1), NL))
        lhalo.append(
            copy(lwin.at[4:8], lwin.at[4 * part : 4 * part + 4], sends.at[8], recvs.at[8], peer)
        )
        lhalo.append(copy(geo, lgeos_v.at[part], sends.at[12], recvs.at[12], peer))
        phalo.append(copy(pwin.at[1], pwin.at[part], sends.at[6], recvs.at[6], peer))
        phalo.append(copy(mwin.at[1], mwin.at[part], sends.at[7], recvs.at[7], peer))

    lane = lax.broadcasted_iota(jnp.int32, (RHS, PTS), 1)
    for i in range(3):
        loads[i].wait()
    pieces = []
    for l in range(16):
        cols = slice(l * PTS, (l + 1) * PTS)
        m = jnp.where(lane < counts[l], rhs_s[:, cols], 0.0)
        mwin[1, :, cols] = m
        pieces.append(nt(m, basis[l]))
    for i in range(3, 8):
        loads[i].wait()
    srow = lax.broadcasted_iota(jnp.int32, (128, 128), 0) >> 4
    blk = block_of((128, 128))
    total = jnp.zeros((128, RANK), jnp.float32)
    for q in range(4):
        tile = jnp.concatenate(pieces[4 * q : 4 * q + 4], axis=1)
        lwin[4 + q] = tile
        own = jnp.full((128, 128), owner[0, 4 * q], jnp.int32)
        for b in range(1, 4):
            own = jnp.where(blk == b, owner[0, 4 * q + b], own)
        lhs = jnp.where(own == srow, jnp.concatenate([tile] * 8, axis=0), 0.0)
        total = total + nn(lhs, leaf_t[4 * q : 4 * q + 4].reshape(128, RANK))
    srow = lax.broadcasted_iota(jnp.int32, (256, 128), 0) >> 4
    blk = block_of((256, 128))
    topp = jnp.zeros((256, RANK), jnp.float32)
    for q in range(2):
        tile = jnp.concatenate(
            [total[(4 * q + b) * 16 : (4 * q + b + 1) * 16] for b in range(4)], axis=1
        )
        midc[q] = tile
        own = jnp.full((256, 128), parent[0, 4 * q], jnp.int32)
        for b in range(1, 4):
            own = jnp.where(blk == b, parent[0, 4 * q + b], own)
        lhs = jnp.where(own == srow, jnp.concatenate([tile] * 16, axis=0), 0.0)
        topp = topp + nn(lhs, mid_t[4 * q : 4 * q + 4].reshape(128, RANK))
    for q in range(4):
        tile = jnp.concatenate(
            [topp[(4 * q + b) * 16 : (4 * q + b + 1) * 16] for b in range(4)], axis=1
        )
        for i in range(8):
            ptop[q * 8 + i] = tile[2 * i : 2 * i + 2]

    for i in range(8, 17):
        loads[i].wait()
    lane1 = lax.broadcasted_iota(jnp.int32, (1, 128), 1)
    row = jnp.zeros((1, 128), jnp.float32)
    for c in range(4):
        for i in range(8):
            row = jnp.where(lane1 == c * 8 + i, mgeo[c, i], row)
        for i in range(16):
            row = jnp.where(lane1 == 32 + c * 16 + i, lgeo[c, i], row)
    geo[...] = row
    geos_v[d] = row
    lgeos_v[1] = row
    row = jnp.zeros((1, 128), jnp.float32)
    for c in range(4):
        for i in range(16):
            row = jnp.where(lane1 == c * 16 + i, ggeo[c, i], row)
    tgeo[...] = row
    tgeos_v[g] = row

    sub = lax.broadcasted_iota(jnp.int32, (8, PTS), 0)

    def split3(v):
        a = bf(v).astype(jnp.float32)
        r = v - a
        b = bf(r).astype(jnp.float32)
        return a, b, r - b

    def window(part, i):
        cols = pl.ds(pl.multiple_of(i * PTS, PTS), PTS)
        m = mwin[part, :, cols]
        high = bf(m)
        w = part * 16 + i
        mhl[w] = jnp.concatenate([high, bf(m - high.astype(jnp.float32))], axis=0)
        c = (pwin[part, :, cols] - 0.5) * RATE
        norm = jnp.sum(c * c, axis=0, keepdims=True)
        c8 = jnp.concatenate([c, jnp.zeros((5, PTS), jnp.float32)], axis=0)
        v = jnp.where(sub == 3, norm, jnp.where(sub == 4, 1.0, c8))
        a, b, e = split3(v)
        bwin[w] = bf(jnp.concatenate([a, a, a, b, b, e], axis=0))
        if part == 1:
            v = jnp.where(sub == 3, 1.0, jnp.where(sub == 4, norm, -2.0 * c8))
            a, b, e = split3(v)
            awin[i] = bf(jnp.concatenate([a, b, e, a, b, a], axis=0).T)

    loop(16, 4, lambda i: window(1, i))

    pl.semaphore_wait(barrier, 62)
    others(NZ, lambda a, b: rs_copy(a, b).start())
    each(1, NG, lambda k: tg_copy(k).start())
    for c in lhalo:
        c.start()
    for c in phalo:
        c.start()
    others(NZ, lambda a, b: geo_copy(a, b).start())
    ring(lambda k: mid_copy(0, k).start())
    for k in range(1, NX):
        mid_copy(1, k).start()
    mids[x * NZ + z] = midc[0]
    mids[NL + z * NX + x] = midc[1]

    def distances(l, sb):
        for j in range(4):
            ws = [l + 16 + partners[l, 2 * j + e] for e in range(2)]
            sb[j] = raw(awin[l], jnp.concatenate([bwin[w] for w in ws], axis=1), 1, 0)

    def kernels(sb, kb):
        for j in range(4):
            k = kappa(sb[j])
            high = bf(k)
            kb[0:PTS, 2 * PTS * j : 2 * PTS * (j + 1)] = high
            kb[PTS : 2 * PTS, 2 * PTS * j : 2 * PTS * (j + 1)] = bf(k - high.astype(jnp.float32))

    def products(l, kb):
        m = jnp.concatenate([mhl[l + 16 + partners[l, j]] for j in range(8)], axis=1)
        acc = raw(m, kb[...], 1, 1)
        base_s[l] = acc[:RHS, :PTS] + (acc[RHS:, :PTS] + acc[:RHS, PTS:])

    def near(i):
        distances(jnp.minimum(2 * i + 2, 15), sb0)
        kernels(sb1, kb1)
        products(2 * i, kb0)
        distances(jnp.minimum(2 * i + 3, 15), sb1)
        kernels(sb0, kb0)
        products(2 * i + 1, kb1)

    blk16 = block_of((RHS, 128))
    blk1 = block_of((1, 128))

    def gather(tab, srcs):
        acc = None
        for j, s in enumerate(srcs):
            t = pltpu.roll(tab[s >> 2], ((j - (s & 3)) & 3) * 32, 1)
            acc = t if j == 0 else jnp.where(blk16 == j, t, acc)
        return acc

    def target_nodes(read):
        h = read(3)
        return [(read(c) + h * tcol[c]) * RATE for c in range(3)]

    def coupling(tnodes, reads):
        def mix(c):
            v = jnp.full((1, 128), reads[0](c), jnp.float32)
            for j in range(1, 4):
                v = jnp.where(blk1 == j, reads[j](c), v)
            return v

        h = mix(3)
        squared = None
        for c in range(3):
            r = (mix(c) + h * trow[c : c + 1, :]) * RATE
            diff = tnodes[c] - r
            squared = diff * diff if squared is None else squared + diff * diff
        return kappa(squared)

    def top_read(s):
        return lambda c: tgeos[s >> 4, 0, c * 16 + (s & 15)]

    def mid_read(i):
        return lambda c: geos[i >> 3, 0, c * 8 + (i & 7)]

    def leaf_read(w):
        return lambda c: lgeos[w >> 4, 0, 32 + c * 16 + (w & 15)]

    def make_w(l):
        w_h[l], w_l[l] = split(dot3(leaf_t[l], basis[l], 0, 0))

    loop(16, 4, make_w)

    got(3)
    to_smem = pltpu.make_async_copy(tgeos_v, tgeos, s_in.at[1])
    to_smem.start()
    to_smem.wait()

    def top_sources(b):
        p = parent[0, b]
        t = g * 16 + p
        return t, [[(t + offsets[p, 4 * q + j]) & 127 for j in range(4)] for q in range(4)]

    def top_coupling(b):
        t, srcs = top_sources(b)
        nodes = target_nodes(top_read(t))
        s = [coupling(nodes, [top_read(i) for i in four]) for four in srcs]
        p_h[b], p_l[b] = split(nn(mid_t[b], jnp.concatenate(s, axis=1)))

    loop(8, 4, top_coupling)

    got(8)
    got(12)
    to_smem = pltpu.make_async_copy(lgeos_v, lgeos, s_in.at[0])
    to_smem.start()
    to_smem.wait()
    def leaf_far(l):
        nodes = target_nodes(leaf_read(l + 16))
        cs, ss = [], []
        for q in range(2):
            srcs = [l + 16 + partners[l, 8 + 4 * q + j] for j in range(4)]
            cs.append(gather(lwin, srcs))
            ss.append(coupling(nodes, [leaf_read(s) for s in srcs]))
        local = nt(jnp.concatenate(cs, axis=1), jnp.concatenate(ss, axis=1))
        far_l[l] = nn(local, basis[l])

    def leaf_four(q):
        for e in range(4):
            leaf_far(4 * q + e)

    each(0, 1, leaf_four)
    got(0)
    terms = [ptop[x * 8 + z]] + [rsbuf[k] for k in range(1, NL)]
    while len(terms) > 1:
        terms = [a + b for a, b in zip(terms[::2], terms[1::2])]
    zbuf[z] = terms[0]
    ring(lambda k: z_copy(k).start())
    got(2)
    got(9)
    for k in range(1, NX):
        mid_copy(2, k).start()
    ring(lambda k: mid_copy(3, k).start())
    each(1, 4, leaf_four)
    got(6)
    got(7)
    loop(16, 4, lambda i: window(0, i))
    loop(16, 4, lambda i: window(2, i))
    distances(0, sb0)
    kernels(sb0, kb0)
    distances(1, sb1)
    each(0, N2, near)
    got(4)
    for i in range(8):
        ztile[2 * i : 2 * i + 2] = zbuf[i]
    others(-1, lambda a, b: top_copy(a, b).start())
    tops[g * NX + x] = ztile[...]
    each(N2, 8, near)

    got(1)
    to_smem = pltpu.make_async_copy(geos_v, geos, s_in.at[0])
    to_smem.start()
    to_smem.wait()

    got(10)
    got(11)

    def mid_coupling(b):
        nodes = target_nodes(mid_read(d * 8 + b))
        cs, ss = [], []
        for q in range(2):
            named = [(peers[b, 4 * q + j], slots[b, 4 * q + j]) for j in range(4)]
            srcs = [p * 8 + i for p, i in named]
            places = [
                jnp.where(i < 4, (p & 3) * NZ + (p >> 2), NL + p) * 4 + (i & 3) for p, i in named
            ]
            cs.append(gather(mids, places))
            ss.append(coupling(nodes, [mid_read(s) for s in srcs]))
        far_m[b] = nt(jnp.concatenate(cs, axis=1), jnp.concatenate(ss, axis=1))

    loop(8, 4, mid_coupling)

    got(5)

    def down_mid(b):
        _, srcs = top_sources(b)
        c = jnp.concatenate([gather(tops, four) for four in srcs], axis=1)
        mid_s[b] = far_m[b] + dot3_split(c, p_h[b], p_l[b], 1, 1)

    loop(8, 8, down_mid)

    for l in range(16):
        cols = slice(l * PTS, (l + 1) * PTS)
        value = base_s[l] + far_l[l] + dot3_split(mid_s[owner[0, l]], w_h[l], w_l[l], 1, 0)
        out[:, cols] = jnp.where(lane < counts[l], value, 0.0)

    for i in range(13):
        sent(i)


N2 = 1
VM = pl.BlockSpec(memory_space=pltpu.VMEM)
ANY = pl.BlockSpec(memory_space=pl.ANY)


def on_device(
    points, rhs, counts, basis, leaf_geom, leaf_partners, leaf_middle_owner, leaf_basis_transfer,
    mid_geom, mid_parent, mid_transfer, mid_peers, mid_slots, top_geom, top_offsets,
):
    table = node_table()
    trow = np.zeros((8, 128), np.float32)
    trow[:3] = np.tile(table, (1, 4))
    tcol = np.broadcast_to(table[:, :, None], (3, 32, 128)).astype(np.float32)
    dma = pltpu.SemaphoreType.DMA

    def vm(*shape, dtype=jnp.float32):
        return pltpu.VMEM(shape, dtype)

    def sm(*shape, dtype=jnp.int32):
        return pltpu.SMEM(shape, dtype)

    product = pl.pallas_call(
        whole_kernel,
        out_shape=pltpu.VMEM((16, 2048), jnp.float32),
        in_specs=[ANY] * 17,
        out_specs=VM,
        scratch_shapes=[
            sm(16), sm(1, 16), sm(1, 8), sm(16, 16), sm(8, 8), sm(8, 8), sm(16, 16),
            sm(4, 8, dtype=jnp.float32), sm(4, 16, dtype=jnp.float32),
            sm(4, 16, dtype=jnp.float32), vm(8, 128), vm(3, 32, 128),
            vm(16, 2048), vm(16, 32, 128), vm(16, 32, 32), vm(8, 32, 32),
            vm(3, 16, 2048), vm(3, 3, 2048), vm(12, 16, 128), vm(2, 16, 128), vm(32, 2, 128),
            vm(1, 128), vm(1, 128),
            vm(64, 16, 128), pltpu.SMEM((32, 1, 128), jnp.float32),
            pltpu.SMEM((8, 1, 128), jnp.float32),
            pltpu.SMEM((3, 1, 128), jnp.float32), vm(32, 16, 128),
            vm(32, 2, 128), vm(8, 2, 128), vm(16, 128),
            vm(48, 32, 128, dtype=jnp.bfloat16), vm(16, 128, 48, dtype=jnp.bfloat16),
            vm(48, 48, 128, dtype=jnp.bfloat16), vm(4, 128, 256), vm(4, 128, 256),
            vm(256, 1024, dtype=jnp.bfloat16),
            vm(256, 1024, dtype=jnp.bfloat16),
            vm(16, 16, 128), vm(16, 16, 128), vm(8, 16, 32), vm(8, 32, 512, dtype=jnp.bfloat16),
            vm(8, 32, 512, dtype=jnp.bfloat16), vm(16, 32, 128, dtype=jnp.bfloat16),
            vm(16, 32, 128, dtype=jnp.bfloat16), vm(8, 16, 32),
            vm(32, 1, 128), vm(8, 1, 128), vm(3, 1, 128),
            dma((17,)), dma((13,)), dma((13,)),
        ],
        compiler_params=pltpu.CompilerParams(collective_id=0, has_side_effects=True),
        name="whole",
    )(
        counts, leaf_middle_owner, mid_parent, leaf_partners, mid_peers, mid_slots, top_offsets,
        mid_geom.T, leaf_geom.T, top_geom.T,
        points, rhs, jnp.swapaxes(basis, 1, 2), leaf_basis_transfer, mid_transfer,
        jnp.asarray(trow), jnp.asarray(tcol),
    )
    return pl.pallas_call(
        store_kernel,
        out_shape=jax.ShapeDtypeStruct((16, 2048), jnp.float32),
        in_specs=[VM],
        out_specs=ANY,
        scratch_shapes=[dma((2,))],
        name="store",
    )(pltpu.with_memory_space_constraint(product, pltpu.VMEM))


def solution(mesh):
    both = ("group", "leaf")
    placed = (
        P(None, both), P(None, both), P(both), P(both, None, None), P(both, None), P(both, None),
        P(both, None), P(both, None, None), P(both, None), P("group", "leaf"), P(both, None, None),
        P(both, None), P(both, None), P("group", None), P("group", None),
    )
    return jax.shard_map(
        on_device, mesh=mesh, in_specs=placed, out_specs=P(None, both), check_vma=False
    )
```

```python
import functools

import jax
import jax.numpy as jnp
import numpy as np
from jax import lax
from jax.experimental import pallas as pl
from jax.experimental.pallas import tpu as pltpu
from jax.sharding import PartitionSpec as P

MESH = pl.DeviceIdType.MESH
PTS = 128
RANK = 32
RHS = 16
RATE = 1.7320508075688772 / 0.5
NX = 4
NZ = 8
NL = 32
NG = 8


def node_table():
    k = np.arange(RANK)
    rows = [
        np.cos(np.pi * (((k * (2 * d + 3)) % RANK) + 0.5) / RANK) for d in range(3)
    ]
    return np.stack(rows).astype(np.float32)


def bf(a):
    return a.astype(jnp.bfloat16)


def raw(a, b, ca, cb):
    return lax.dot_general(
        a, b, (((ca,), (cb,)), ((), ())), preferred_element_type=jnp.float32
    )


def dot3(a, b, ca, cb):
    ah, bh = bf(a), bf(b)
    al, bl = bf(a - ah.astype(jnp.float32)), bf(b - bh.astype(jnp.float32))
    return raw(ah, bh, ca, cb) + (raw(al, bh, ca, cb) + raw(ah, bl, ca, cb))


def split(a):
    high = bf(a)
    return high, bf(a - high.astype(jnp.float32))


def dot3_split(a, bh, bl, ca, cb):
    ah, al = split(a)
    return raw(ah, bh, ca, cb) + (raw(al, bh, ca, cb) + raw(ah, bl, ca, cb))


def nt(a, b):
    return dot3(a, b, 1, 1)


def nn(a, b):
    return dot3(a, b, 1, 0)


def kappa(squared):
    squared = jnp.maximum(squared, 1e-30)
    t = squared * lax.rsqrt(squared)
    return (1.0 + t) * jnp.exp2(t * -1.4426950408889634)


def block_of(shape):
    return lax.broadcasted_iota(jnp.int32, shape, 1) >> 5


def loop(count, width, f):
    def step(i, c):
        for e in range(width):
            f(i * width + e)
        return c

    lax.fori_loop(0, count // width, step, 0)


def store_kernel(product, out, sems):
    parts = [
        pltpu.make_async_copy(product.at[8 * i : 8 * i + 8], out.at[8 * i : 8 * i + 8], sems.at[i])
        for i in range(2)
    ]
    for c in parts:
        c.start()
    for c in parts:
        c.wait()


def whole_kernel(
    counts_h, owner_h, parent_h, partners_h, peers_h, slots_h, offsets_h, mgeo_h, lgeo_h, ggeo_h,
    points, rhs, basis_h, leaf_h, mid_h, trow_h, tcol_h,
    out,
    counts, owner, parent, partners, peers, slots, offsets, mgeo, lgeo, ggeo, trow, tcol,
    rhs_s, basis, leaf_t, mid_t, mwin, pwin, lwin, midc, ptop, geo, tgeo,
    mids, geos, tgeos, lgeos, tops, rsbuf, zbuf, ztile,
    mhl, awin, bwin, sb0, sb1, kb0, kb1, base_s, far_l, far_m, p_h, p_l, w_h, w_l, mid_s, geos_v, tgeos_v, lgeos_v,
    s_in, sends, recvs,
):
    g = lax.axis_index("group")
    d = lax.axis_index("leaf")
    z = d // NX
    x = d % NX

    y = g // 2
    core = g % 2
    xs = [x] + [lax.rem(x + b, NX) for b in range(1, NX)]
    zs = [z] + [lax.rem(z + a, NZ) for a in range(1, NZ)]
    ys = [y] + [lax.rem(y + a, 4) for a in range(1, 4)]
    cs = [core, 1 - core]

    def leaf_peer(a, b):
        return (g, zs[a] * NX + xs[b])

    def plane_peer(a, b):
        return (ys[a // 2] * 2 + cs[a % 2], z * NX + xs[b])

    def each(lo, hi, f):
        def step(k, c):
            f(k)
            return c

        lax.fori_loop(lo, hi, step, 0)

    def others(count, f):
        def hops(a, b):
            along = min(a, NZ - a) if count == NZ else min(a // 2, 4 - a // 2)
            return along + min(b, NX - b)

        pairs = [(a, b) for a in range(8) for b in range(NX) if (a, b) != (0, 0)]
        for a, b in sorted(pairs, key=lambda p: -hops(*p)):
            f(a, b)

    barrier = pltpu.get_barrier_semaphore()

    def hello(peer):
        pl.semaphore_signal(barrier, inc=1, device_id=peer, device_id_type=MESH)

    others(-1, lambda a, b: hello(plane_peer(a, b)))
    others(NZ, lambda a, b: hello(leaf_peer(a, b)))

    loads = [
        pltpu.make_async_copy(a, b, s_in.at[i])
        for i, (a, b) in enumerate(
            [
                (counts_h, counts), (rhs, rhs_s), (basis_h, basis), (owner_h, owner),
                (parent_h, parent), (leaf_h, leaf_t), (mid_h, mid_t), (points, pwin.at[1]),
                (mgeo_h, mgeo), (lgeo_h, lgeo), (ggeo_h, ggeo),
                (partners_h, partners), (peers_h, peers), (slots_h, slots),
                (offsets_h, offsets), (trow_h, trow), (tcol_h, tcol),
            ]
        )
    ]
    for c in loads:
        c.start()

    def copy(src, dst, ss, rs, peer):
        return pltpu.make_async_remote_copy(
            src_ref=src, dst_ref=dst, send_sem=ss, recv_sem=rs, device_id=peer, device_id_type=MESH
        )

    def rs_copy(a, b):
        piece = ptop.at[xs[b] * NZ + zs[a]]
        return copy(piece, rsbuf.at[a * NX + b], sends.at[0], recvs.at[0], leaf_peer(a, b))

    def geo_copy(a, b):
        return copy(geo, geos_v.at[d], sends.at[1], recvs.at[1], leaf_peer(a, b))

    def mid_copy(step, k):
        if step == 0:
            i = x * NZ + z
            return copy(midc.at[0], mids.at[i], sends.at[2], recvs.at[2], leaf_peer(k, 0))
        if step == 1:
            i = NL + z * NX + x
            return copy(midc.at[1], mids.at[i], sends.at[9], recvs.at[9], leaf_peer(0, k))
        if step == 2:
            block = mids.at[pl.ds(x * NZ, NZ)]
            return copy(block, block, sends.at[10], recvs.at[10], leaf_peer(0, k))
        block = mids.at[pl.ds(NL + z * NX, NX)]
        return copy(block, block, sends.at[11], recvs.at[11], leaf_peer(k, 0))

    def tg_copy(k):
        return copy(tgeo, tgeos_v.at[g], sends.at[3], recvs.at[3], (lax.rem(g + k, NG), d))

    def z_copy(k):
        return copy(zbuf.at[z], zbuf.at[z], sends.at[4], recvs.at[4], leaf_peer(k, 0))

    def ring(f):
        for k in (4, 3, 5, 2, 6, 1, 7):
            f(k)

    def top_copy(a, b):
        return copy(ztile, tops.at[g * NX + x], sends.at[5], recvs.at[5], plane_peer(a, b))

    whole = [
        rsbuf.at[pl.ds(1, NL - 1)], geos_v.at[pl.ds(0, NL - 1)], mids.at[pl.ds(0, NZ - 1)],
        tgeos_v.at[pl.ds(0, NG - 1)], zbuf.at[pl.ds(0, NZ - 1)], tops.at[pl.ds(0, 31)],
        pwin.at[pl.ds(0, 2)], mwin.at[pl.ds(0, 2)], lwin.at[pl.ds(0, 8)],
        mids.at[pl.ds(0, NX - 1)], mids.at[pl.ds(0, NZ * (NX - 1))],
        mids.at[pl.ds(0, NX * (NZ - 1))], lgeos_v.at[pl.ds(0, 2)],
    ]

    def got(i):
        pltpu.make_async_copy(whole[i], whole[i], recvs.at[i]).wait()

    def sent(i):
        pltpu.make_async_copy(whole[i], whole[i], sends.at[i]).wait()

    lhalo, phalo = [], []
    for side in range(2):
        part = 2 - 2 * side
        peer = (g, lax.rem(d + (NL - 1 if side == 0 else 1), NL))
        lhalo.append(
            copy(lwin.at[4:8], lwin.at[4 * part : 4 * part + 4], sends.at[8], recvs.at[8], peer)
        )
        lhalo.append(copy(geo, lgeos_v.at[part], sends.at[12], recvs.at[12], peer))
        phalo.append(copy(pwin.at[1], pwin.at[part], sends.at[6], recvs.at[6], peer))
        phalo.append(copy(mwin.at[1], mwin.at[part], sends.at[7], recvs.at[7], peer))

    lane = lax.broadcasted_iota(jnp.int32, (RHS, PTS), 1)
    for i in range(3):
        loads[i].wait()
    pieces = []
    for l in range(16):
        cols = slice(l * PTS, (l + 1) * PTS)
        m = jnp.where(lane < counts[l], rhs_s[:, cols], 0.0)
        mwin[1, :, cols] = m
        pieces.append(nt(m, basis[l]))
    for i in range(3, 8):
        loads[i].wait()
    srow = lax.broadcasted_iota(jnp.int32, (128, 128), 0) >> 4
    blk = block_of((128, 128))
    total = jnp.zeros((128, RANK), jnp.float32)
    for q in range(4):
        tile = jnp.concatenate(pieces[4 * q : 4 * q + 4], axis=1)
        lwin[4 + q] = tile
        own = jnp.full((128, 128), owner[0, 4 * q], jnp.int32)
        for b in range(1, 4):
            own = jnp.where(blk == b, owner[0, 4 * q + b], own)
        lhs = jnp.where(own == srow, jnp.concatenate([tile] * 8, axis=0), 0.0)
        total = total + nn(lhs, leaf_t[4 * q : 4 * q + 4].reshape(128, RANK))
    srow = lax.broadcasted_iota(jnp.int32, (256, 128), 0) >> 4
    blk = block_of((256, 128))
    topp = jnp.zeros((256, RANK), jnp.float32)
    for q in range(2):
        tile = jnp.concatenate(
            [total[(4 * q + b) * 16 : (4 * q + b + 1) * 16] for b in range(4)], axis=1
        )
        midc[q] = tile
        own = jnp.full((256, 128), parent[0, 4 * q], jnp.int32)
        for b in range(1, 4):
            own = jnp.where(blk == b, parent[0, 4 * q + b], own)
        lhs = jnp.where(own == srow, jnp.concatenate([tile] * 16, axis=0), 0.0)
        topp = topp + nn(lhs, mid_t[4 * q : 4 * q + 4].reshape(128, RANK))
    for q in range(4):
        tile = jnp.concatenate(
            [topp[(4 * q + b) * 16 : (4 * q + b + 1) * 16] for b in range(4)], axis=1
        )
        for i in range(8):
            ptop[q * 8 + i] = tile[2 * i : 2 * i + 2]

    for i in range(8, 17):
        loads[i].wait()
    lane1 = lax.broadcasted_iota(jnp.int32, (1, 128), 1)
    row = jnp.zeros((1, 128), jnp.float32)
    for c in range(4):
        for i in range(8):
            row = jnp.where(lane1 == i * 4 + c, mgeo[c, i], row)
        for i in range(16):
            row = jnp.where(lane1 == 32 + i * 4 + c, lgeo[c, i], row)
    geo[...] = row
    geos_v[d] = row
    lgeos_v[1] = row
    row = jnp.zeros((1, 128), jnp.float32)
    for c in range(4):
        for i in range(16):
            row = jnp.where(lane1 == i * 4 + c, ggeo[c, i], row)
    tgeo[...] = row
    tgeos_v[g] = row

    sub = lax.broadcasted_iota(jnp.int32, (8, PTS), 0)

    def split3(v):
        a = bf(v).astype(jnp.float32)
        r = v - a
        b = bf(r).astype(jnp.float32)
        return a, b, r - b

    def window(part, i):
        cols = pl.ds(pl.multiple_of(i * PTS, PTS), PTS)
        m = mwin[part, :, cols]
        high = bf(m)
        w = part * 16 + i
        mhl[w] = jnp.concatenate([high, bf(m - high.astype(jnp.float32))], axis=0)
        c = (pwin[part, :, cols] - 0.5) * RATE
        norm = jnp.sum(c * c, axis=0, keepdims=True)
        c8 = jnp.concatenate([c, jnp.zeros((5, PTS), jnp.float32)], axis=0)
        v = jnp.where(sub == 3, norm, jnp.where(sub == 4, 1.0, c8))
        a, b, e = split3(v)
        bwin[w] = bf(jnp.concatenate([a, a, a, b, b, e], axis=0))
        if part == 1:
            v = jnp.where(sub == 3, 1.0, jnp.where(sub == 4, norm, -2.0 * c8))
            a, b, e = split3(v)
            awin[i] = bf(jnp.concatenate([a, b, e, a, b, a], axis=0).T)

    loop(16, 4, lambda i: window(1, i))

    pl.semaphore_wait(barrier, 62)
    others(NZ, lambda a, b: rs_copy(a, b).start())
    each(1, NG, lambda k: tg_copy(k).start())
    for c in lhalo:
        c.start()
    for c in phalo:
        c.start()
    others(NZ, lambda a, b: geo_copy(a, b).start())
    ring(lambda k: mid_copy(0, k).start())
    for k in range(1, NX):
        mid_copy(1, k).start()
    mids[x * NZ + z] = midc[0]
    mids[NL + z * NX + x] = midc[1]

    def distances(l, sb):
        for j in range(4):
            ws = [l + 16 + partners[l, 2 * j + e] for e in range(2)]
            sb[j] = raw(awin[l], jnp.concatenate([bwin[w] for w in ws], axis=1), 1, 0)

    def kernels(sb, kb):
        for j in range(4):
            k = kappa(sb[j])
            high = bf(k)
            kb[0:PTS, 2 * PTS * j : 2 * PTS * (j + 1)] = high
            kb[PTS : 2 * PTS, 2 * PTS * j : 2 * PTS * (j + 1)] = bf(k - high.astype(jnp.float32))

    def products(l, kb):
        m = jnp.concatenate([mhl[l + 16 + partners[l, j]] for j in range(8)], axis=1)
        acc = raw(m, kb[...], 1, 1)
        base_s[l] = acc[:RHS, :PTS] + (acc[RHS:, :PTS] + acc[:RHS, PTS:])

    def near(i):
        distances(jnp.minimum(2 * i + 2, 15), sb0)
        kernels(sb1, kb1)
        products(2 * i, kb0)
        distances(jnp.minimum(2 * i + 3, 15), sb1)
        kernels(sb0, kb0)
        products(2 * i + 1, kb1)

    blk16 = block_of((RHS, 128))
    blk1 = block_of((1, 128))

    def gather(tab, srcs):
        acc = None
        for j, s in enumerate(srcs):
            t = pltpu.roll(tab[s >> 2], ((j - (s & 3)) & 3) * 32, 1)
            acc = t if j == 0 else jnp.where(blk16 == j, t, acc)
        return acc

    def target_nodes(read):
        h = read(3)
        return [(read(c) + h * tcol[c]) * RATE for c in range(3)]

    def coupling(tnodes, reads):
        def mix(c):
            v = jnp.full((1, 128), reads[0](c), jnp.float32)
            for j in range(1, 4):
                v = jnp.where(blk1 == j, reads[j](c), v)
            return v

        h = mix(3)
        squared = None
        for c in range(3):
            r = (mix(c) + h * trow[c : c + 1, :]) * RATE
            diff = tnodes[c] - r
            squared = diff * diff if squared is None else squared + diff * diff
        return kappa(squared)

    def top_read(s):
        return lambda c: tgeos[s >> 4, 0, (s & 15) * 4 + c]

    def mid_read(i):
        return lambda c: geos[i >> 3, 0, (i & 7) * 4 + c]

    def leaf_read(w):
        return lambda c: lgeos[w >> 4, 0, 32 + (w & 15) * 4 + c]

    def make_w(l):
        w_h[l], w_l[l] = split(dot3(leaf_t[l], basis[l], 0, 0))

    loop(16, 4, make_w)

    got(3)
    to_smem = pltpu.make_async_copy(tgeos_v, tgeos, s_in.at[1])
    to_smem.start()
    to_smem.wait()

    def top_sources(b):
        p = parent[0, b]
        t = g * 16 + p
        return t, [[(t + offsets[p, 4 * q + j]) & 127 for j in range(4)] for q in range(4)]

    def top_coupling(b):
        t, srcs = top_sources(b)
        nodes = target_nodes(top_read(t))
        s = [coupling(nodes, [top_read(i) for i in four]) for four in srcs]
        p_h[b], p_l[b] = split(nn(mid_t[b], jnp.concatenate(s, axis=1)))

    loop(8, 4, top_coupling)

    got(8)
    got(12)
    to_smem = pltpu.make_async_copy(lgeos_v, lgeos, s_in.at[0])
    to_smem.start()
    to_smem.wait()
    def leaf_far(l):
        nodes = target_nodes(leaf_read(l + 16))
        cs, ss = [], []
        for q in range(2):
            srcs = [l + 16 + partners[l, 8 + 4 * q + j] for j in range(4)]
            cs.append(gather(lwin, srcs))
            ss.append(coupling(nodes, [leaf_read(s) for s in srcs]))
        local = nt(jnp.concatenate(cs, axis=1), jnp.concatenate(ss, axis=1))
        far_l[l] = nn(local, basis[l])

    def leaf_four(q):
        for e in range(4):
            leaf_far(4 * q + e)

    each(0, 1, leaf_four)
    got(0)
    terms = [ptop[x * 8 + z]] + [rsbuf[k] for k in range(1, NL)]
    while len(terms) > 1:
        terms = [a + b for a, b in zip(terms[::2], terms[1::2])]
    zbuf[z] = terms[0]
    ring(lambda k: z_copy(k).start())
    got(2)
    got(9)
    for k in range(1, NX):
        mid_copy(2, k).start()
    ring(lambda k: mid_copy(3, k).start())
    each(1, 4, leaf_four)
    got(6)
    got(7)
    loop(16, 4, lambda i: window(0, i))
    loop(16, 4, lambda i: window(2, i))
    distances(0, sb0)
    kernels(sb0, kb0)
    distances(1, sb1)
    each(0, N2, near)
    got(4)
    for i in range(8):
        ztile[2 * i : 2 * i + 2] = zbuf[i]
    others(-1, lambda a, b: top_copy(a, b).start())
    tops[g * NX + x] = ztile[...]
    each(N2, 8, near)

    got(1)
    to_smem = pltpu.make_async_copy(geos_v, geos, s_in.at[0])
    to_smem.start()
    to_smem.wait()

    got(10)
    got(11)

    def mid_coupling(b):
        nodes = target_nodes(mid_read(d * 8 + b))
        cs, ss = [], []
        for q in range(2):
            named = [(peers[b, 4 * q + j], slots[b, 4 * q + j]) for j in range(4)]
            srcs = [p * 8 + i for p, i in named]
            places = [
                jnp.where(i < 4, (p & 3) * NZ + (p >> 2), NL + p) * 4 + (i & 3) for p, i in named
            ]
            cs.append(gather(mids, places))
            ss.append(coupling(nodes, [mid_read(s) for s in srcs]))
        far_m[b] = nt(jnp.concatenate(cs, axis=1), jnp.concatenate(ss, axis=1))

    loop(8, 4, mid_coupling)

    got(5)

    def down_mid(b):
        _, srcs = top_sources(b)
        c = jnp.concatenate([gather(tops, four) for four in srcs], axis=1)
        mid_s[b] = far_m[b] + dot3_split(c, p_h[b], p_l[b], 1, 1)

    loop(8, 8, down_mid)

    for l in range(16):
        cols = slice(l * PTS, (l + 1) * PTS)
        value = base_s[l] + far_l[l] + dot3_split(mid_s[owner[0, l]], w_h[l], w_l[l], 1, 0)
        out[:, cols] = jnp.where(lane < counts[l], value, 0.0)

    for i in range(13):
        sent(i)


N2 = 1
VM = pl.BlockSpec(memory_space=pltpu.VMEM)
ANY = pl.BlockSpec(memory_space=pl.ANY)


def on_device(
    points, rhs, counts, basis, leaf_geom, leaf_partners, leaf_middle_owner, leaf_basis_transfer,
    mid_geom, mid_parent, mid_transfer, mid_peers, mid_slots, top_geom, top_offsets,
):
    table = node_table()
    trow = np.zeros((8, 128), np.float32)
    trow[:3] = np.tile(table, (1, 4))
    tcol = np.broadcast_to(table[:, :, None], (3, 32, 128)).astype(np.float32)
    dma = pltpu.SemaphoreType.DMA

    def vm(*shape, dtype=jnp.float32):
        return pltpu.VMEM(shape, dtype)

    def sm(*shape, dtype=jnp.int32):
        return pltpu.SMEM(shape, dtype)

    product = pl.pallas_call(
        whole_kernel,
        out_shape=pltpu.VMEM((16, 2048), jnp.float32),
        in_specs=[ANY] * 17,
        out_specs=VM,
        scratch_shapes=[
            sm(16), sm(1, 16), sm(1, 8), sm(16, 16), sm(8, 8), sm(8, 8), sm(16, 16),
            sm(4, 8, dtype=jnp.float32), sm(4, 16, dtype=jnp.float32),
            sm(4, 16, dtype=jnp.float32), vm(8, 128), vm(3, 32, 128),
            vm(16, 2048), vm(16, 32, 128), vm(16, 32, 32), vm(8, 32, 32),
            vm(3, 16, 2048), vm(3, 3, 2048), vm(12, 16, 128), vm(2, 16, 128), vm(32, 2, 128),
            vm(1, 128), vm(1, 128),
            vm(64, 16, 128), pltpu.SMEM((32, 1, 128), jnp.float32),
            pltpu.SMEM((8, 1, 128), jnp.float32),
            pltpu.SMEM((3, 1, 128), jnp.float32), vm(32, 16, 128),
            vm(32, 2, 128), vm(8, 2, 128), vm(16, 128),
            vm(48, 32, 128, dtype=jnp.bfloat16), vm(16, 128, 48, dtype=jnp.bfloat16),
            vm(48, 48, 128, dtype=jnp.bfloat16), vm(4, 128, 256), vm(4, 128, 256),
            vm(256, 1024, dtype=jnp.bfloat16),
            vm(256, 1024, dtype=jnp.bfloat16),
            vm(16, 16, 128), vm(16, 16, 128), vm(8, 16, 32), vm(8, 32, 512, dtype=jnp.bfloat16),
            vm(8, 32, 512, dtype=jnp.bfloat16), vm(16, 32, 128, dtype=jnp.bfloat16),
            vm(16, 32, 128, dtype=jnp.bfloat16), vm(8, 16, 32),
            vm(32, 1, 128), vm(8, 1, 128), vm(3, 1, 128),
            dma((17,)), dma((13,)), dma((13,)),
        ],
        compiler_params=pltpu.CompilerParams(collective_id=0, has_side_effects=True),
        name="whole",
    )(
        counts, leaf_middle_owner, mid_parent, leaf_partners, mid_peers, mid_slots, top_offsets,
        mid_geom.T, leaf_geom.T, top_geom.T,
        points, rhs, jnp.swapaxes(basis, 1, 2), leaf_basis_transfer, mid_transfer,
        jnp.asarray(trow), jnp.asarray(tcol),
    )
    return pl.pallas_call(
        store_kernel,
        out_shape=jax.ShapeDtypeStruct((16, 2048), jnp.float32),
        in_specs=[VM],
        out_specs=ANY,
        scratch_shapes=[dma((2,))],
        name="store",
    )(pltpu.with_memory_space_constraint(product, pltpu.VMEM))


def solution(mesh):
    both = ("group", "leaf")
    placed = (
        P(None, both), P(None, both), P(both), P(both, None, None), P(both, None), P(both, None),
        P(both, None), P(both, None, None), P(both, None), P("group", "leaf"), P(both, None, None),
        P(both, None), P(both, None), P("group", None), P("group", None),
    )
    return jax.shard_map(
        on_device, mesh=mesh, in_specs=placed, out_specs=P(None, both), check_vma=False
    )
```
